32 devices in a mesh: row: 8 (over y, x, core), col: 4 (over z).
Axes of the slice: x: 2, y: 2, z: 4, core: 2. Of those that a mesh axis runs over, the one named last changes fastest.
Arguments:
- matrix: float32 [8, 3, 256, 4, 6, 256], P('row', None, None, 'col'), as said below
- checksum: float32 [8, 3, 256, 6, 256], P('row'), as said below
- failed: int32 [4], P('col'), may hold values from 0 to 3, as said below
Outputs:
- factored: float32 [8, 3, 256, 4, 6, 256], P('row', None, None, 'col')
- updated_checksum_result: float32 [8, 3, 256, 6, 256], P('row')
The draws below stay inside these ranges and needn't reach their ends.
Inputs may be any that keep to these rules, and one draw needn't show every extreme that they name: `failed`: a permutation of the grid column indices; entry 0 names the grid column whose tiles in matrix carry no information. With the lost grid column rebuilt from checksum, matrix is symmetric positive definite. `checksum`: for each grid row, the sum over all grid columns of the intact matrix's tiles, the lost column included.
All inputs are finite; a program needn't handle non-finite values.
Results may differ from the reference program's by a relative error of at most 0.0003.
Values sent between devices are 32-bit elements; how exact they have to be, the bound alone decides.
A program may use at most 128 MiB of HBM per device.

```python
import math
import jax
import jax.numpy as jnp
from jax import lax

B = 256
PANELS = 3
GRID_ROWS = 8
GRID_COLS = 4
NT = 24
TR = 3
TC = 6
ORDER = 6144


def intact_tiles(key):
    full_order = NT * B
    inner_width = 2 * B
    loadings = jax.random.normal(jax.random.fold_in(key, 5), (full_order, inner_width), jnp.float32)
    loadings = loadings / math.sqrt(inner_width)
    square = 2.0 * jnp.dot(loadings, loadings.T, precision=lax.Precision.HIGHEST)
    diagonal_lift = jax.random.uniform(jax.random.fold_in(key, 6), (full_order,), jnp.float32, 0.5, 1.5)
    square = square + jnp.diag(diagonal_lift)
    return square.reshape(TR, GRID_ROWS, B, TC, GRID_COLS, B).transpose(1, 0, 2, 4, 3, 5)


def column_order(key):
    return jax.random.permutation(jax.random.fold_in(key, 4517), jnp.arange(GRID_COLS, dtype=jnp.int32))


def draw_failed(key, part):
    return column_order(key)


def draw_matrix(key, part):
    blocks = intact_tiles(key)
    garbage = jax.random.normal(jax.random.fold_in(key, 7), blocks.shape, jnp.float32)
    column_ids = jnp.arange(GRID_COLS, dtype=jnp.int32).reshape(1, 1, 1, GRID_COLS, 1, 1)
    return jnp.where(column_ids == column_order(key)[0], garbage, blocks)


def draw_checksum(key, part):
    return jnp.sum(intact_tiles(key), axis=3)


def setup_inputs(seed: int = 0) -> dict:
    streams_of = jax.random.split(jax.random.key(seed), 4)
    return {
        "matrix": draw_matrix(jax.random.fold_in(streams_of[3], 71), 0),
        "checksum": draw_checksum(jax.random.fold_in(streams_of[3], 71), 0),
        "failed": draw_failed(jax.random.fold_in(streams_of[3], 71), 0),
    }


def to_natural(blocks):
    return blocks.transpose(1, 0, 2, 4, 3, 5).reshape(ORDER, ORDER)

def split_into_tiles(square):
    return square.reshape(TR, GRID_ROWS, B, TC, GRID_COLS, B).transpose(1, 0, 2, 4, 3, 5)

def reference(matrix, checksum, failed):
    missing_tiles = failed[0]
    column_ids = jnp.arange(GRID_COLS, dtype=jnp.int32).reshape(1, 1, 1, GRID_COLS, 1, 1)
    remaining_peers = jnp.sum(jnp.where(column_ids != missing_tiles, matrix, 0.0), axis=3)
    restored_tiles = jnp.where(column_ids == missing_tiles, (checksum - remaining_peers)[:, :, :, None], matrix)
    work = to_natural(restored_tiles)
    columns = []
    for panel in range(PANELS):
        start = panel * B
        factor = jnp.linalg.cholesky(work[start:start + B, start:start + B])
        below = work[start + B:, start:start + B]
        solved = jax.scipy.linalg.solve_triangular(factor, below.T, lower=True).T
        upper_zero = jnp.zeros((start, B), work.dtype)
        block_column = jnp.concatenate([upper_zero, factor, solved], axis=0)
        work = work - jnp.dot(block_column, block_column.T, precision=lax.Precision.HIGHEST)
        columns.append(block_column)
    tiles = split_into_tiles(work)
    updated_checksum_result = jnp.sum(tiles, axis=3)
    for panel in range(PANELS):
        panel_tiles = columns[panel].reshape(TR, GRID_ROWS, B, B).transpose(1, 0, 2, 3)
        tiles = tiles.at[:, :, :, panel % GRID_COLS, panel // GRID_COLS, :].set(panel_tiles)
    tile_rows = jnp.arange(GRID_ROWS)[:, None] + jnp.arange(TR)[None, :] * GRID_ROWS
    tile_cols = jnp.arange(GRID_COLS)[:, None] + jnp.arange(TC)[None, :] * GRID_COLS
    keep = tile_rows.reshape(GRID_ROWS, TR, 1, 1, 1, 1) >= tile_cols.reshape(1, 1, 1, GRID_COLS, TC, 1)
    factored = jnp.where(keep, tiles, 0.0)
    return (factored, updated_checksum_result)
```

```python
import functools

import jax
import jax.numpy as jnp
from jax import lax
from jax.experimental import pallas as pl
from jax.experimental.pallas import tpu as pltpu
from jax.sharding import PartitionSpec as P

PANELS = 3
BLOCK = 128
EXACT = lax.Precision.HIGHEST
MESH = pl.DeviceIdType.MESH
F32 = jnp.float32
BF16 = jnp.bfloat16


def exact_dot(a, b, ca, cb):
    return lax.dot_general(
        a, b, (((ca,), (cb,)), ((), ())), precision=EXACT, preferred_element_type=F32
    )


def split(x):
    high = x.astype(BF16)
    return high, (x - high.astype(F32)).astype(BF16)


def dot3(a, b, ca, cb):
    dims = (((ca,), (cb,)), ((), ()))
    make = lambda x, y: lax.dot_general(x, y, dims, preferred_element_type=F32)
    return make(a[0], b[0]) + (make(a[0], b[1]) + make(a[1], b[0]))


def factor_block(block):
    n = block.shape[0]
    groups = n // 8
    rows = lax.broadcasted_iota(jnp.int32, (8, n), 0)
    lanes = lax.broadcasted_iota(jnp.int32, (8, n), 1)
    a = [block[8 * h : 8 * h + 8, :] for h in range(groups)]
    m = [jnp.where(lanes == rows + 8 * h, 1.0, 0.0).astype(F32) for h in range(groups)]
    lane = lambda x, j: jnp.broadcast_to(x[:, j : j + 1], (8, n))
    row = lambda x, j: jnp.broadcast_to(x[j : j + 1, :], (8, n))
    for g in range(groups):
        cols = [[lane(a[h], 8 * g + l) for l in range(8)] for h in range(g, groups)]
        for j in range(8):
            scale = lax.rsqrt(row(cols[0][j], j))
            a_row = row(a[g], j) * scale
            m_row = row(m[g], j) * scale
            heads = [row(cols[0][l], j) * scale for l in range(j + 1, 8)]
            for h in range(g, groups):
                c = cols[h - g][j] * scale
                if h == g:
                    below = jnp.where(rows > j, c, 0.0)
                    a[h] = jnp.where(rows == j, a_row, a[h] - below * a_row)
                    m[h] = jnp.where(rows == j, m_row, m[h] - below * m_row)
                else:
                    a[h] = a[h] - c * a_row
                    m[h] = m[h] - c * m_row
                for l in range(j + 1, 8):
                    cols[h - g][l] = cols[h - g][l] - c * heads[l - j - 1]
    upper = jnp.concatenate(a, axis=0)
    inverse = jnp.concatenate(m, axis=0)
    r = lax.broadcasted_iota(jnp.int32, (n, n), 0)
    c = lax.broadcasted_iota(jnp.int32, (n, n), 1)
    return jnp.where(r <= c, upper, 0.0).T, jnp.where(r >= c, inverse, 0.0)


def bit(value, b):
    return lax.rem(value // (2**b), 2)


def all_of(conditions):
    return functools.reduce(jnp.logical_and, conditions)


def plan(rows_count, cols_count, tile_rows, tile_cols):
    need = [min(tile_cols, (rows_count * (a + 1) - 1) // cols_count + 1) for a in range(tile_rows)]
    return need, [(a, b) for a in range(tile_rows) for b in range(1, need[a])]


def kernel(
    rows_count, cols_count,
    own, totals, flag,
    work, new_totals,
    flags, gathered, panel, lead, factor, inverses, inv_tile, cross, sums,
    left_in, right_in, left_out, right_out, low_high, low_low,
    flag_send, flag_recv, gather_send, gather_recv, scan_send, scan_recv, cast_send, cast_recv,
):
    tile_rows, tile_cols, width, _ = own.shape
    p, q = lax.axis_index("row"), lax.axis_index("col")
    last = cols_count - 1
    bits = rows_count.bit_length() - 1
    need, tiles = plan(rows_count, cols_count, tile_rows, tile_cols)
    ratio = rows_count // cols_count
    wide = PANELS * width

    barrier = pltpu.get_barrier_semaphore()
    for o in range(cols_count):
        @pl.when(q != o)
        def _():
            pl.semaphore_signal(barrier, inc=1, device_id=(p, jnp.int32(o)), device_id_type=MESH)
    partners = [p + (1 - 2 * bit(p, b)) * (2**b) for b in range(bits)]
    for partner in partners:
        pl.semaphore_signal(barrier, inc=1, device_id=(partner, q), device_id_type=MESH)
    pl.semaphore_wait(barrier, cols_count - 1 + bits)

    def remote(src, dst, send, recv, to):
        return pltpu.make_async_remote_copy(
            src_ref=src, dst_ref=dst, send_sem=send, recv_sem=recv, device_id=to, device_id_type=MESH
        )

    def flag_copy(o):
        return remote(flag, flags, flag_send.at[o], flag_recv, (p, jnp.int32(o)))

    def flag_start():
        @pl.when(q == 0)
        def _():
            for o in range(1, cols_count):
                flag_copy(o).start()
            flags[...] = flag[...]

    def flag_wait():
        @pl.when(q != 0)
        def _():
            flag_copy(0).wait_recv()

    def lost_is(index, shape):
        return jnp.broadcast_to(flags[0:1, 0:1], shape) == index

    sides = (0, 1)
    ahead = [jnp.minimum(q + 1, last), jnp.maximum(q - 1, 0)]

    def gather_copy(side, step, a, origin):
        at = gathered.at[origin, a]
        return remote(at, at, gather_send.at[side, step, a], gather_recv.at[side, step, a], (p, ahead[side]))

    def gather_sends(side, step):
        if side == 0:
            return jnp.logical_and(q - step >= 0, q < last), jnp.maximum(q - step, 0)
        return jnp.logical_and(q + step <= last, q > 0), jnp.minimum(q + step, last)

    def gather_gets(side, step):
        if side == 0:
            return q - 1 - step >= 0, jnp.maximum(q - 1 - step, 0)
        return q + 1 + step <= last, jnp.minimum(q + 1 + step, last)

    def gather_start(step, a):
        for side in sides:
            does, origin = gather_sends(side, step)
            @pl.when(does)
            def _():
                gather_copy(side, step, a, origin).start()

    def gather_wait(step, a):
        for side in sides:
            does, origin = gather_gets(side, step)
            @pl.when(does)
            def _():
                gather_copy(side, step, a, origin).wait_recv()

    def rebuild_panel(a):
        shape = (width, width)
        others = jnp.zeros(shape, F32)
        for o in range(cols_count):
            others = others + jnp.where(lost_is(o, shape), 0.0, gathered[o, a])
        patch = totals[a, 0] - others
        for k in range(PANELS):
            panel[a, :, k * width : (k + 1) * width] = jnp.where(lost_is(k, shape), patch, gathered[k, a])
        work[a, 0] = jnp.where(lost_is(q, shape), patch, own[a, 0])

    forth = [b for b in range(1, bits)] + [0]
    back = [b for b in range(bits - 1, 0, -1)] + [0]

    class Cast:
        def __init__(self, number, buffer, source, order):
            self.number, self.buffer, self.order = number, buffer, order
            self.apart = [lax.rem(bit(p, b) + bit(source, b), 2) for b in range(bits)]
            self.is_source = p == source

        def copy(self, t):
            return remote(
                self.buffer, self.buffer, cast_send.at[self.number, t], cast_recv.at[self.number],
                (partners[self.order[t]], q),
            )

        def holds(self, t):
            return all_of([self.apart[b] == 0 for b in self.order[t:]])

        def gets(self, t):
            return all_of(
                [self.apart[self.order[t]] == 1] + [self.apart[b] == 0 for b in self.order[t + 1 :]]
            )

        def start(self, t):
            @pl.when(self.holds(t))
            def _():
                self.copy(t).start()

        def wait(self, t):
            @pl.when(self.gets(t))
            def _():
                self.copy(t).wait_recv()

        def finish(self):
            for t in range(bits):
                @pl.when(self.holds(t))
                def _():
                    self.copy(t).wait_send()

    number = iter(range(64))
    lead_casts = [
        Cast(next(number), lead.at[i * width : (i + 1) * width, 0 : (i + 1) * width], jnp.int32(i), back)
        for i in range(PANELS)
    ]
    sum_casts = [Cast(next(number), sums.at[k * width : (k + 1) * width], jnp.int32(k), forth) for k in range(PANELS)]
    cross_casts = [Cast(next(number), cross.at[m], q + cols_count * m, back) for m in range(ratio)]

    def cast_start(casts, t):
        for cast in casts:
            cast.start(t)

    def cast_wait(casts, t):
        for cast in casts:
            cast.wait(t)

    def lead_stage():
        for i, cast in enumerate(lead_casts):
            @pl.when(cast.is_source)
            def _():
                top = slice(0, (i + 1) * width)
                lead[i * width : (i + 1) * width, top] = panel[0, :, top]

    def sum_stage():
        for k, cast in enumerate(sum_casts):
            @pl.when(cast.is_source)
            def _():
                for b in range(tile_cols):
                    sums[k * width : (k + 1) * width, b * width : (b + 1) * width] = totals[0, b]

    def cross_stage():
        for m, cast in enumerate(cross_casts):
            @pl.when(cast.is_source)
            def _():
                for a in range(tile_rows):
                    cross[m, a] = panel[a]

    scan_in, scan_out = (left_in, right_in), (left_out, right_out)
    scan_ends = (0, last)

    def scan_copy(side, t, first):
        a, b = tiles[t]
        src = own.at[a, b] if first else scan_out[side].at[t]
        return remote(src, scan_in[side].at[t], scan_send.at[side, t], scan_recv.at[side, t], (p, ahead[side]))

    def scan_first(t):
        for side in sides:
            @pl.when(q == scan_ends[side])
            def _():
                scan_copy(side, t, True).start()

    def scan_next(t):
        a, b = tiles[t]
        for side in sides:
            @pl.when(jnp.logical_and(q > 0, q < last))
            def _():
                scan_copy(side, t, False).wait_recv()
                scan_out[side][t] = scan_in[side][t] + own[a, b]
                scan_copy(side, t, False).start()

    def scan_last(t):
        for side in sides:
            @pl.when(q == scan_ends[1 - side])
            def _():
                scan_copy(side, t, False).wait_recv()
            @pl.when(q == scan_ends[side])
            def _():
                scan_in[side][t] = jnp.zeros((width, width), F32)

    def finish():
        @pl.when(q == 0)
        def _():
            for o in range(1, cols_count):
                flag_copy(o).wait_send()
        for step in range(last):
            for a in range(tile_rows):
                for side in sides:
                    does, origin = gather_sends(side, step)
                    @pl.when(does)
                    def _():
                        gather_copy(side, step, a, origin).wait_send()
        for t in range(len(tiles)):
            for side in sides:
                @pl.when(q != scan_ends[1 - side])
                def _():
                    scan_copy(side, t, False).wait_send()
        for cast in sum_casts + cross_casts:
            cast.finish()

    for i in range(PANELS - 1):
        lead[i * width : (i + 1) * width, (i + 1) * width :] = jnp.zeros((width, wide - (i + 1) * width), F32)
    rest = range(1, tile_rows)
    flag_start()
    for a in range(tile_rows):
        gathered[q, a] = own[a, 0]
    gather_start(0, 0)
    sum_stage()
    cast_start(sum_casts, 0)
    for step in range(last):
        gather_wait(step, 0)
        if step + 1 < last:
            gather_start(step + 1, 0)
        if step == 0:
            for a in rest:
                gather_start(0, a)
    flag_wait()
    rebuild_panel(0)
    lead_stage()
    cast_start(lead_casts, 0)
    for t in range(bits):
        cast_wait(lead_casts, t)
        if t + 1 < bits:
            cast_start(lead_casts, t + 1)

    def gather_rest(step):
        for a in rest:
            gather_wait(step, a)
            if step + 1 < last:
                gather_start(step + 1, a)

    def cross_begin():
        for a in rest:
            rebuild_panel(a)
        cross_stage()
        cast_start(cross_casts, 0)

    def cast_step(casts, t):
        cast_wait(casts, t)
        if t + 1 < bits:
            cast_start(casts, t + 1)

    count = len(tiles)
    third = -(-count // 3)
    chunks = [range(min(count, third * c), min(count, third * (c + 1))) for c in range(3)]

    def each(fn, ts):
        for t in ts:
            fn(t)

    blocks = wide // BLOCK
    service = [[] for _ in range(blocks)]
    service[0] = [lambda: gather_rest(0), lambda: each(scan_first, range(count))]
    service[1] = [lambda step=step: gather_rest(step) for step in range(1, last)] + [cross_begin]
    service[2] = [lambda: cast_step(sum_casts, 0)]
    service[3] = [lambda: each(scan_next, chunks[0])]
    service[4] = [lambda: cast_step(cross_casts, 0), lambda: cast_step(sum_casts, 1)]
    service[5] = [lambda: each(scan_next, chunks[1])]

    block_rows = lax.broadcasted_iota(jnp.int32, (wide, BLOCK), 0)

    def factor_step(n, carry):
        for at in range(blocks):
            @pl.when(n == at)
            def _():
                for action in service[at]:
                    action()
        o = pl.multiple_of(n * BLOCK, BLOCK)
        lower, inverse = factor_block(lead[pl.ds(o, BLOCK), pl.ds(o, BLOCK)])
        below = exact_dot(lead[:, pl.ds(o, BLOCK)], inverse, 1, 1)
        below = jnp.where(block_rows >= o + BLOCK, below, 0.0)
        lead[...] = lead[...] - exact_dot(below, below, 1, 1)
        factor[:, pl.ds(o, BLOCK)] = below
        factor[pl.ds(o, BLOCK), pl.ds(o, BLOCK)] = lower
        inverses[n] = inverse
        return carry

    for cast in lead_casts:
        cast.finish()
    lax.fori_loop(0, blocks, factor_step, 0)

    for k in range(PANELS):
        one, two = inverses[2 * k], inverses[2 * k + 1]
        corner = factor[k * width + BLOCK : (k + 1) * width, k * width : k * width + BLOCK]
        inv_tile[k, :BLOCK, :BLOCK] = one
        inv_tile[k, :BLOCK, BLOCK:] = jnp.zeros((BLOCK, BLOCK), F32)
        inv_tile[k, BLOCK:, :BLOCK] = -exact_dot(two, exact_dot(corner, one, 1, 0), 1, 0)
        inv_tile[k, BLOCK:, BLOCK:] = two

    def part(i, m):
        return split(factor[i * width : (i + 1) * width, m * width : (m + 1) * width])

    def solve_rows(x):
        solved = []
        for k in range(PANELS):
            y = x[:, k * width : (k + 1) * width]
            for m in range(k):
                y = y - dot3(split(solved[m]), part(k, m), 1, 1)
            solved.append(dot3(split(y), split(inv_tile[k]), 1, 1))
        return jnp.concatenate(solved, axis=1)

    row_tile = [p + a * rows_count for a in range(tile_rows)]

    def rows_body(a, carry):
        x = solve_rows(panel[a])
        take = jnp.logical_and(a == 0, p < PANELS)
        top = factor[pl.ds(pl.multiple_of(jnp.minimum(p, PANELS - 1) * width, width), width), :]
        pick = jnp.broadcast_to(jnp.where(take, 1, 0), x.shape) == 1
        x = jnp.where(pick, top, x)
        panel[a] = x
        low_high[a], low_low[a] = split(x)
        return carry

    lax.fori_loop(0, tile_rows, rows_body, 0)

    cast_step(sum_casts, 2)
    for t in range(3, bits):
        cast_step(sum_casts, t)

    def sums_body(b, carry):
        at = pl.ds(pl.multiple_of(b * width, width), width)
        solved = []
        for k in range(PANELS):
            y = sums[k * width : (k + 1) * width, at]
            for m in range(k):
                y = y - dot3(part(k, m), solved[m], 1, 0)
            solved.append(split(dot3(split(inv_tile[k]), split(y), 1, 0)))
        y = (jnp.concatenate([s[0] for s in solved], 0), jnp.concatenate([s[1] for s in solved], 0))
        for a in range(tile_rows):
            new_totals[a, b] = totals[a, b] - dot3((low_high[a], low_low[a]), y, 1, 0)
        return carry

    lax.fori_loop(0, tile_cols, sums_body, 0)

    for t in range(1, bits):
        cast_step(cross_casts, t)
    each(scan_next, chunks[2])
    each(scan_last, range(count))

    shape = (width, width)

    def finish_tile(a, b, y):
        value = dot3((low_high[a], low_low[a]), y, 1, 1)
        if b == 0:
            value = work[a, 0] - value
            for k in range(PANELS):
                value = jnp.where(
                    jnp.broadcast_to(q, shape) == k, panel[a, :, k * width : (k + 1) * width], value
                )
        else:
            t = tiles.index((a, b))
            back_in = totals[a, b] - (left_in[t] + right_in[t])
            value = jnp.where(lost_is(q, shape), back_in, own[a, b]) - value
        keep = jnp.broadcast_to(row_tile[a], shape) >= jnp.broadcast_to(q + b * cols_count, shape)
        work[a, b] = jnp.where(keep, value, 0.0)

    for b in range(tile_cols):
        m, a_from = b % ratio, b // ratio
        y = split(solve_rows(cross[m, a_from]))
        for a in range(tile_rows):
            if b < need[a]:
                finish_tile(a, b, y)
            else:
                work[a, b] = jnp.zeros(shape, F32)
    finish()


def shards(matrix, checksum, failed):
    rows_count, cols_count = lax.axis_size("row"), lax.axis_size("col")
    tile_rows, width, tile_cols = matrix.shape[1], matrix.shape[2], matrix.shape[4]
    assert width == 2 * BLOCK and rows_count % cols_count == 0
    assert cols_count >= PANELS and rows_count & (rows_count - 1) == 0
    own = matrix.reshape(tile_rows, width, tile_cols, width).transpose(0, 2, 1, 3)
    totals = checksum.reshape(tile_rows, width, tile_cols, width).transpose(0, 2, 1, 3)
    flag = jnp.broadcast_to(failed.reshape(1, 1), (8, 128))
    wide = PANELS * width
    bits = rows_count.bit_length() - 1
    ratio = rows_count // cols_count
    _, tiles = plan(rows_count, cols_count, tile_rows, tile_cols)
    count = len(tiles)
    casts = 2 * PANELS + ratio
    vmem = pl.BlockSpec(memory_space=pltpu.VMEM)
    dma = pltpu.SemaphoreType.DMA
    result = jax.ShapeDtypeStruct(own.shape, F32)
    work, new_totals = pl.pallas_call(
        functools.partial(kernel, rows_count, cols_count),
        out_shape=[result, result],
        in_specs=[vmem] * 3,
        out_specs=[vmem] * 2,
        scratch_shapes=[
            pltpu.VMEM((8, 128), jnp.int32),
            pltpu.VMEM((cols_count, tile_rows, width, width), F32),
            pltpu.VMEM((tile_rows, width, wide), F32),
            pltpu.VMEM((wide, wide), F32),
            pltpu.VMEM((wide, wide), F32),
            pltpu.VMEM((wide // BLOCK, BLOCK, BLOCK), F32),
            pltpu.VMEM((PANELS, width, width), F32),
            pltpu.VMEM((ratio, tile_rows, width, wide), F32),
            pltpu.VMEM((wide, tile_cols * width), F32),
        ]
        + [pltpu.VMEM((count, width, width), F32)] * 4
        + [pltpu.VMEM((tile_rows, width, wide), BF16)] * 2
        + [
            dma((cols_count,)),
            dma,
            dma((2, cols_count - 1, tile_rows)),
            dma((2, cols_count - 1, tile_rows)),
            dma((2, count)),
            dma((2, count)),
            dma((casts, bits)),
            dma((casts,)),
        ],
        compiler_params=pltpu.CompilerParams(
            collective_id=0, has_side_effects=True, vmem_limit_bytes=62 * 2**20
        ),
        cost_estimate=pl.CostEstimate(flops=30 * 10**9, bytes_accessed=20 * 10**6, transcendentals=0),
    )(own, totals, flag)
    work = work.transpose(0, 2, 1, 3)
    new_totals = new_totals.transpose(0, 2, 1, 3)
    return work.reshape(matrix.shape), new_totals.reshape(checksum.shape)


def solution(mesh):
    return jax.shard_map(
        shards,
        mesh=mesh,
        in_specs=(
            P("row", None, None, "col", None, None),
            P("row", None, None, None, None),
            P("col"),
        ),
        out_specs=(P("row", None, None, "col", None, None), P("row", None, None, None, None)),
        check_vma=False,
    )
```

```python
import functools

import jax
import jax.numpy as jnp
from jax import lax
from jax.experimental import pallas as pl
from jax.experimental.pallas import tpu as pltpu
from jax.sharding import PartitionSpec as P

PANELS = 3
BLOCK = 128
EXACT = lax.Precision.HIGHEST
MESH = pl.DeviceIdType.MESH
F32 = jnp.float32
BF16 = jnp.bfloat16


def exact_dot(a, b, ca, cb):
    return lax.dot_general(
        a, b, (((ca,), (cb,)), ((), ())), precision=EXACT, preferred_element_type=F32
    )


def split(x):
    high = x.astype(BF16)
    return high, (x - high.astype(F32)).astype(BF16)


def dot3(a, b, ca, cb):
    dims = (((ca,), (cb,)), ((), ()))
    make = lambda x, y: lax.dot_general(x, y, dims, preferred_element_type=F32)
    return make(a[0], b[0]) + (make(a[0], b[1]) + make(a[1], b[0]))


def factor_block(block, middle):
    n = block.shape[0]
    groups = n // 8
    rows = lax.broadcasted_iota(jnp.int32, (8, n), 0)
    lanes = lax.broadcasted_iota(jnp.int32, (8, n), 1)
    a = [block[8 * h : 8 * h + 8, :] for h in range(groups)]
    m = [jnp.where(lanes == rows + 8 * h, 1.0, 0.0).astype(F32) for h in range(groups)]
    lane = lambda x, j: jnp.broadcast_to(x[:, j : j + 1], (8, n))
    row = lambda x, j: jnp.broadcast_to(x[j : j + 1, :], (8, n))
    for g in range(groups):
        if g == groups // 2:
            middle()
        cols = [[lane(a[h], 8 * g + l) for l in range(8)] for h in range(g, groups)]
        for j in range(8):
            scale = lax.rsqrt(row(cols[0][j], j))
            a_row = row(a[g], j) * scale
            m_row = row(m[g], j) * scale
            heads = [row(cols[0][l], j) * scale for l in range(j + 1, 8)]
            for h in range(g, groups):
                c = cols[h - g][j] * scale
                if h == g:
                    below = jnp.where(rows > j, c, 0.0)
                    a[h] = jnp.where(rows == j, a_row, a[h] - below * a_row)
                    m[h] = jnp.where(rows == j, m_row, m[h] - below * m_row)
                else:
                    a[h] = a[h] - c * a_row
                    m[h] = m[h] - c * m_row
                for l in range(j + 1, 8):
                    cols[h - g][l] = cols[h - g][l] - c * heads[l - j - 1]
    upper = jnp.concatenate(a, axis=0)
    inverse = jnp.concatenate(m, axis=0)
    r = lax.broadcasted_iota(jnp.int32, (n, n), 0)
    c = lax.broadcasted_iota(jnp.int32, (n, n), 1)
    return jnp.where(r <= c, upper, 0.0).T, jnp.where(r >= c, inverse, 0.0)


def bit(value, b):
    return lax.rem(value // (2**b), 2)


def all_of(conditions):
    return functools.reduce(jnp.logical_and, conditions)


def plan(rows_count, cols_count, tile_rows, tile_cols):
    need = [min(tile_cols, (rows_count * (a + 1) - 1) // cols_count + 1) for a in range(tile_rows)]
    return need, [(a, b) for a in range(tile_rows) for b in range(1, need[a])]


def kernel(
    rows_count, cols_count,
    own, totals, flag,
    work, new_totals,
    flags, gathered, panel, lead, factor, inverses, inv_tile, cross, sums,
    left_in, right_in, left_out, right_out, low_high, low_low, front,
    flag_send, flag_recv, gather_send, gather_recv, scan_send, scan_recv, cast_send, cast_recv,
):
    tile_rows, tile_cols, width, _ = totals.shape
    p, q = lax.axis_index("row"), lax.axis_index("col")
    last = cols_count - 1
    bits = rows_count.bit_length() - 1
    need, tiles = plan(rows_count, cols_count, tile_rows, tile_cols)
    ratio = rows_count // cols_count
    wide = PANELS * width

    barrier = pltpu.get_barrier_semaphore()
    for o in range(cols_count):
        @pl.when(q != o)
        def _():
            pl.semaphore_signal(barrier, inc=1, device_id=(p, jnp.int32(o)), device_id_type=MESH)
    partners = [p + (1 - 2 * bit(p, b)) * (2**b) for b in range(bits)]
    for partner in partners:
        pl.semaphore_signal(barrier, inc=1, device_id=(partner, q), device_id_type=MESH)
    pl.semaphore_wait(barrier, cols_count - 1 + bits)

    def remote(src, dst, send, recv, to):
        return pltpu.make_async_remote_copy(
            src_ref=src, dst_ref=dst, send_sem=send, recv_sem=recv, device_id=to, device_id_type=MESH
        )

    def flag_copy(o):
        return remote(flag, flags, flag_send.at[o], flag_recv, (p, jnp.int32(o)))

    def flag_start():
        @pl.when(q == 0)
        def _():
            for o in range(1, cols_count):
                flag_copy(o).start()
            flags[...] = flag[...]

    def flag_wait():
        @pl.when(q != 0)
        def _():
            flag_copy(0).wait_recv()

    def lost_is(index, shape):
        return jnp.broadcast_to(flags[0:1, 0:1], shape) == index

    sides = (0, 1)
    ahead = [jnp.minimum(q + 1, last), jnp.maximum(q - 1, 0)]

    def gather_copy(side, step, a, origin):
        at = gathered.at[origin, a]
        return remote(at, at, gather_send.at[side, step, a], gather_recv.at[side, step, a], (p, ahead[side]))

    def gather_sends(side, step):
        if side == 0:
            return jnp.logical_and(q - step >= 0, q < last), jnp.maximum(q - step, 0)
        return jnp.logical_and(q + step <= last, q > 0), jnp.minimum(q + step, last)

    def gather_gets(side, step):
        if side == 0:
            return q - 1 - step >= 0, jnp.maximum(q - 1 - step, 0)
        return q + 1 + step <= last, jnp.minimum(q + 1 + step, last)

    def gather_start(step, a):
        for side in sides:
            does, origin = gather_sends(side, step)
            @pl.when(does)
            def _():
                gather_copy(side, step, a, origin).start()

    def gather_wait(step, a):
        for side in sides:
            does, origin = gather_gets(side, step)
            @pl.when(does)
            def _():
                gather_copy(side, step, a, origin).wait_recv()

    def rebuild_panel(a):
        shape = (width, width)
        others = jnp.zeros(shape, F32)
        for o in range(cols_count):
            others = others + jnp.where(lost_is(o, shape), 0.0, gathered[o, a])
        patch = totals[a, 0] - others
        for k in range(PANELS):
            panel[a, :, k * width : (k + 1) * width] = jnp.where(lost_is(k, shape), patch, gathered[k, a])
        front[a] = jnp.where(lost_is(q, shape), patch, own[a * tile_cols])

    forth = [b for b in range(1, bits)] + [0]
    back = [b for b in range(bits - 1, 0, -1)] + [0]

    class Cast:
        def __init__(self, number, buffer, source, order):
            self.number, self.buffer, self.order = number, buffer, order
            self.apart = [lax.rem(bit(p, b) + bit(source, b), 2) for b in range(bits)]
            self.is_source = p == source

        def copy(self, t):
            return remote(
                self.buffer, self.buffer, cast_send.at[self.number, t], cast_recv.at[self.number],
                (partners[self.order[t]], q),
            )

        def holds(self, t):
            return all_of([self.apart[b] == 0 for b in self.order[t:]])

        def gets(self, t):
            return all_of(
                [self.apart[self.order[t]] == 1] + [self.apart[b] == 0 for b in self.order[t + 1 :]]
            )

        def start(self, t):
            @pl.when(self.holds(t))
            def _():
                self.copy(t).start()

        def wait(self, t):
            @pl.when(self.gets(t))
            def _():
                self.copy(t).wait_recv()

        def finish(self):
            for t in range(bits):
                @pl.when(self.holds(t))
                def _():
                    self.copy(t).wait_send()

    number = iter(range(64))
    lead_casts = [
        Cast(next(number), lead.at[i * width : (i + 1) * width, 0 : (i + 1) * width], jnp.int32(i), back)
        for i in range(PANELS)
    ]
    orders = (forth, back)
    half = width // 2
    sum_casts = [
        Cast(next(number), sums.at[k * width + h * half : k * width + (h + 1) * half], jnp.int32(k), orders[h])
        for k in range(PANELS)
        for h in range(2)
    ]
    cross_casts = [
        Cast(next(number), cross.at[m, :, h * half : (h + 1) * half], q + cols_count * m, orders[h])
        for m in range(ratio)
        for h in range(2)
    ]

    def cast_start(casts, t):
        for cast in casts:
            cast.start(t)

    def cast_wait(casts, t):
        for cast in casts:
            cast.wait(t)

    def lead_stage():
        for i, cast in enumerate(lead_casts):
            @pl.when(cast.is_source)
            def _():
                top = slice(0, (i + 1) * width)
                lead[i * width : (i + 1) * width, top] = panel[0, :, top]

    def sum_stage():
        for k, cast in enumerate(sum_casts[::2]):
            @pl.when(cast.is_source)
            def _():
                for b in range(tile_cols):
                    sums[k * width : (k + 1) * width, b * width : (b + 1) * width] = totals[0, b]

    def cross_stage():
        for m, cast in enumerate(cross_casts[::2]):
            @pl.when(cast.is_source)
            def _():
                for a in range(tile_rows):
                    cross[m, a] = panel[a]

    scan_in, scan_out = (left_in, right_in), (left_out, right_out)
    scan_ends = (0, last)

    count = len(tiles)
    lag = 2
    hops = (q, last - q)

    def scan_copy(side, t, src):
        return remote(src, scan_in[side].at[t], scan_send.at[side, t], scan_recv.at[side, t], (p, ahead[side]))

    def scan_tick(n):
        for side in sides:
            hop = hops[side]
            t = n - lag * hop
            busy = jnp.logical_and(jnp.logical_and(t >= 0, t < count), hop < last)
            t = jnp.clip(t, 0, count - 1)
            at = jnp.int32(0)
            for i, (a, b) in enumerate(tiles):
                at = jnp.where(t == i, a * tile_cols + b, at)

            @pl.when(jnp.logical_and(busy, hop == 0))
            def _():
                scan_copy(side, t, own.at[at]).start()

            @pl.when(jnp.logical_and(busy, hop > 0))
            def _():
                copy = scan_copy(side, t, scan_out[side].at[t])
                copy.wait_recv()
                scan_out[side][t] = scan_in[side][t] + own[at]
                copy.start()

    def scan_last(t):
        for side in sides:
            @pl.when(q == scan_ends[1 - side])
            def _():
                scan_copy(side, t, scan_out[side].at[t]).wait_recv()
            @pl.when(q == scan_ends[side])
            def _():
                scan_in[side][t] = jnp.zeros((width, width), F32)

    def finish():
        @pl.when(q == 0)
        def _():
            for o in range(1, cols_count):
                flag_copy(o).wait_send()
        for step in range(last):
            for a in range(tile_rows):
                for side in sides:
                    does, origin = gather_sends(side, step)
                    @pl.when(does)
                    def _():
                        gather_copy(side, step, a, origin).wait_send()
        for t in range(len(tiles)):
            for side in sides:
                @pl.when(q != scan_ends[1 - side])
                def _():
                    scan_copy(side, t, scan_out[side].at[t]).wait_send()
        for cast in sum_casts + cross_casts:
            cast.finish()

    for i in range(PANELS - 1):
        lead[i * width : (i + 1) * width, (i + 1) * width :] = jnp.zeros((width, wide - (i + 1) * width), F32)
    rest = range(1, tile_rows)
    flag_start()
    for a in range(tile_rows):
        gathered[q, a] = own[a * tile_cols]
    gather_start(0, 0)
    sum_stage()
    cast_start(sum_casts, 0)
    for step in range(last):
        gather_wait(step, 0)
        if step + 1 < last:
            gather_start(step + 1, 0)
        if step + 2 == last:
            for a in rest:
                gather_start(0, a)
    flag_wait()
    rebuild_panel(0)
    lead_stage()
    cast_start(lead_casts, 0)

    def cast_step(casts, t):
        cast_wait(casts, t)
        if t + 1 < bits:
            cast_start(casts, t + 1)

    def gather_step(step):
        for a in rest:
            gather_wait(step, a)
            if step + 1 < last:
                gather_start(step + 1, a)

    cast_step(sum_casts, 0)
    for t in range(bits):
        cast_step(lead_casts, t)
        if t < min(2, last):
            gather_step(t)

    def cross_begin():
        for a in rest:
            rebuild_panel(a)
        cross_stage()
        cast_start(cross_casts, 0)

    blocks = wide // BLOCK
    service = [[] for _ in range(2 * blocks)]
    service[1] = [lambda step=step: gather_step(step) for step in range(min(bits, 2, last), last)] + [cross_begin]
    service[4] = [lambda: cast_step(sum_casts, 1)]
    service[6] = [lambda: cast_step(cross_casts, 0)]
    first_tick = 1

    def serve(n, at):
        for point in range(at, 2 * blocks, 2):
            if service[point]:
                @pl.when(2 * n + at == point)
                def _():
                    for action in service[point]:
                        action()
        scan_tick(2 * n + at - first_tick)

    block_rows = lax.broadcasted_iota(jnp.int32, (wide, BLOCK), 0)

    def factor_step(n, carry):
        serve(n, 0)
        o = pl.multiple_of(n * BLOCK, BLOCK)
        lower, inverse = factor_block(
            lead[pl.ds(o, BLOCK), pl.ds(o, BLOCK)], lambda: serve(n, 1)
        )
        below = exact_dot(lead[:, pl.ds(o, BLOCK)], inverse, 1, 1)
        below = jnp.where(block_rows >= o + BLOCK, below, 0.0)
        lead[...] = lead[...] - exact_dot(below, below, 1, 1)
        factor[:, pl.ds(o, BLOCK)] = below
        factor[pl.ds(o, BLOCK), pl.ds(o, BLOCK)] = lower
        inverses[n] = inverse
        return carry

    for cast in lead_casts:
        cast.finish()
    lax.fori_loop(0, blocks, factor_step, 0)

    for k in range(PANELS):
        one, two = inverses[2 * k], inverses[2 * k + 1]
        corner = factor[k * width + BLOCK : (k + 1) * width, k * width : k * width + BLOCK]
        inv_tile[k, :BLOCK, :BLOCK] = one
        inv_tile[k, :BLOCK, BLOCK:] = jnp.zeros((BLOCK, BLOCK), F32)
        inv_tile[k, BLOCK:, :BLOCK] = -exact_dot(two, exact_dot(corner, one, 1, 0), 1, 0)
        inv_tile[k, BLOCK:, BLOCK:] = two

    def part(i, m):
        return split(factor[i * width : (i + 1) * width, m * width : (m + 1) * width])

    def solve_rows(x):
        solved = []
        for k in range(PANELS):
            y = x[:, k * width : (k + 1) * width]
            for m in range(k):
                y = y - dot3(split(solved[m]), part(k, m), 1, 1)
            solved.append(dot3(split(y), split(inv_tile[k]), 1, 1))
        return jnp.concatenate(solved, axis=1)

    row_tile = [p + a * rows_count for a in range(tile_rows)]

    def rows_body(a, carry):
        scan_tick(tick + a)
        x = solve_rows(panel[a])
        take = jnp.logical_and(a == 0, p < PANELS)
        top = factor[pl.ds(pl.multiple_of(jnp.minimum(p, PANELS - 1) * width, width), width), :]
        pick = jnp.broadcast_to(jnp.where(take, 1, 0), x.shape) == 1
        x = jnp.where(pick, top, x)
        panel[a] = x
        low_high[a], low_low[a] = split(x)
        return carry

    tick = 2 * blocks - first_tick
    lax.fori_loop(0, tile_rows, rows_body, 0)
    tick += tile_rows

    for t in range(2, bits):
        cast_step(sum_casts, t)
    cast_step(cross_casts, 1)

    def sums_body(b, carry):
        scan_tick(tick + b)
        at = pl.ds(pl.multiple_of(b * width, width), width)
        solved = []
        for k in range(PANELS):
            y = sums[k * width : (k + 1) * width, at]
            for m in range(k):
                y = y - dot3(part(k, m), solved[m], 1, 0)
            solved.append(split(dot3(split(inv_tile[k]), split(y), 1, 0)))
        y = (jnp.concatenate([s[0] for s in solved], 0), jnp.concatenate([s[1] for s in solved], 0))
        for a in range(tile_rows):
            new_totals[a, b] = totals[a, b] - dot3((low_high[a], low_low[a]), y, 1, 0)
        return carry

    lax.fori_loop(0, tile_cols, sums_body, 0)
    tick += tile_cols
    for t in range(2, bits):
        cast_step(cross_casts, t)

    for b in range(tile_cols):
        scan_tick(tick + b)
        y = split(solve_rows(cross[b % ratio, b // ratio]))
        for a in range(tile_rows):
            if b < need[a]:
                work[a, b] = dot3((low_high[a], low_low[a]), y, 1, 1)
    tick += tile_cols
    ticks = count + lag * (last - 1)

    def tick_body(n, carry):
        scan_tick(n)
        return carry

    if ticks > tick:
        lax.fori_loop(tick, ticks, tick_body, 0)
    for t in range(count):
        scan_last(t)

    shape = (width, width)
    for a in range(tile_rows):
        for b in range(tile_cols):
            if b >= need[a]:
                work[a, b] = jnp.zeros(shape, F32)
                continue
            if b == 0:
                value = front[a] - work[a, b]
                for k in range(PANELS):
                    value = jnp.where(
                        jnp.broadcast_to(q, shape) == k, panel[a, :, k * width : (k + 1) * width], value
                    )
            else:
                t = tiles.index((a, b))
                back_in = totals[a, b] - (left_in[t] + right_in[t])
                value = jnp.where(lost_is(q, shape), back_in, own[a * tile_cols + b]) - work[a, b]
            keep = jnp.broadcast_to(row_tile[a], shape) >= jnp.broadcast_to(q + b * cols_count, shape)
            work[a, b] = jnp.where(keep, value, 0.0)
    finish()


def shards(matrix, checksum, failed):
    rows_count, cols_count = lax.axis_size("row"), lax.axis_size("col")
    tile_rows, width, tile_cols = matrix.shape[1], matrix.shape[2], matrix.shape[4]
    assert width == 2 * BLOCK and rows_count % cols_count == 0
    assert cols_count >= PANELS and rows_count & (rows_count - 1) == 0
    own = matrix.reshape(tile_rows, width, tile_cols, width).transpose(0, 2, 1, 3)
    totals = checksum.reshape(tile_rows, width, tile_cols, width).transpose(0, 2, 1, 3)
    flag = jnp.broadcast_to(failed.reshape(1, 1), (8, 128))
    wide = PANELS * width
    bits = rows_count.bit_length() - 1
    ratio = rows_count // cols_count
    _, tiles = plan(rows_count, cols_count, tile_rows, tile_cols)
    count = len(tiles)
    casts = 3 * PANELS + 2 * ratio
    vmem = pl.BlockSpec(memory_space=pltpu.VMEM)
    dma = pltpu.SemaphoreType.DMA
    result = jax.ShapeDtypeStruct(own.shape, F32)
    work, new_totals = pl.pallas_call(
        functools.partial(kernel, rows_count, cols_count),
        out_shape=[result, result],
        in_specs=[vmem] * 3,
        out_specs=[vmem] * 2,
        scratch_shapes=[
            pltpu.VMEM((8, 128), jnp.int32),
            pltpu.VMEM((cols_count, tile_rows, width, width), F32),
            pltpu.VMEM((tile_rows, width, wide), F32),
            pltpu.VMEM((wide, wide), F32),
            pltpu.VMEM((wide, wide), F32),
            pltpu.VMEM((wide // BLOCK, BLOCK, BLOCK), F32),
            pltpu.VMEM((PANELS, width, width), F32),
            pltpu.VMEM((ratio, tile_rows, width, wide), F32),
            pltpu.VMEM((wide, tile_cols * width), F32),
        ]
        + [pltpu.VMEM((count, width, width), F32)] * 4
        + [pltpu.VMEM((tile_rows, width, wide), BF16)] * 2
        + [pltpu.VMEM((tile_rows, width, width), F32)]
        + [
            dma((cols_count,)),
            dma,
            dma((2, cols_count - 1, tile_rows)),
            dma((2, cols_count - 1, tile_rows)),
            dma((2, count)),
            dma((2, count)),
            dma((casts, bits)),
            dma((casts,)),
        ],
        compiler_params=pltpu.CompilerParams(
            collective_id=0, has_side_effects=True, vmem_limit_bytes=62 * 2**20
        ),
        cost_estimate=pl.CostEstimate(flops=30 * 10**9, bytes_accessed=20 * 10**6, transcendentals=0),
    )(own.reshape(-1, width, width), totals, flag)
    work = work.transpose(0, 2, 1, 3)
    new_totals = new_totals.transpose(0, 2, 1, 3)
    return work.reshape(matrix.shape), new_totals.reshape(checksum.shape)


def solution(mesh):
    return jax.shard_map(
        shards,
        mesh=mesh,
        in_specs=(
            P("row", None, None, "col", None, None),
            P("row", None, None, None, None),
            P("col"),
        ),
        out_specs=(P("row", None, None, "col", None, None), P("row", None, None, None, None)),
        check_vma=False,
    )
```

```python
import functools

import jax
import jax.numpy as jnp
from jax import lax
from jax.experimental import pallas as pl
from jax.experimental.pallas import tpu as pltpu
from jax.sharding import PartitionSpec as P

PANELS = 3
BLOCK = 128
EXACT = lax.Precision.HIGHEST
MESH = pl.DeviceIdType.MESH
F32 = jnp.float32
BF16 = jnp.bfloat16


def exact_dot(a, b, ca, cb):
    return lax.dot_general(
        a, b, (((ca,), (cb,)), ((), ())), precision=EXACT, preferred_element_type=F32
    )


def split(x):
    high = x.astype(BF16)
    return high, (x - high.astype(F32)).astype(BF16)


def dot3(a, b, ca, cb):
    dims = (((ca,), (cb,)), ((), ()))
    make = lambda x, y: lax.dot_general(x, y, dims, preferred_element_type=F32)
    return make(a[0], b[0]) + (make(a[0], b[1]) + make(a[1], b[0]))


def factor_block(block, middle):
    n = block.shape[0]
    groups = n // 8
    rows = lax.broadcasted_iota(jnp.int32, (8, n), 0)
    lanes = lax.broadcasted_iota(jnp.int32, (8, n), 1)
    a = [block[8 * h : 8 * h + 8, :] for h in range(groups)]
    m = [jnp.where(lanes == rows + 8 * h, 1.0, 0.0).astype(F32) for h in range(groups)]
    lane = lambda x, j: jnp.broadcast_to(x[:, j : j + 1], (8, n))
    row = lambda x, j: jnp.broadcast_to(x[j : j + 1, :], (8, n))
    for g in range(groups):
        if g == groups // 2:
            middle()
        cols = [[lane(a[h], 8 * g + l) for l in range(8)] for h in range(g, groups)]
        for j in range(8):
            scale = lax.rsqrt(row(cols[0][j], j))
            a_row = row(a[g], j) * scale
            m_row = row(m[g], j) * scale
            heads = [row(cols[0][l], j) * scale for l in range(j + 1, 8)]
            for h in range(g, groups):
                c = cols[h - g][j] * scale
                if h == g:
                    below = jnp.where(rows > j, c, 0.0)
                    a[h] = jnp.where(rows == j, a_row, a[h] - below * a_row)
                    m[h] = jnp.where(rows == j, m_row, m[h] - below * m_row)
                else:
                    a[h] = a[h] - c * a_row
                    m[h] = m[h] - c * m_row
                for l in range(j + 1, 8):
                    cols[h - g][l] = cols[h - g][l] - c * heads[l - j - 1]
    upper = jnp.concatenate(a, axis=0)
    inverse = jnp.concatenate(m, axis=0)
    r = lax.broadcasted_iota(jnp.int32, (n, n), 0)
    c = lax.broadcasted_iota(jnp.int32, (n, n), 1)
    return jnp.where(r <= c, upper, 0.0).T, jnp.where(r >= c, inverse, 0.0)


def bit(value, b):
    return lax.rem(value // (2**b), 2)


def all_of(conditions):
    return functools.reduce(jnp.logical_and, conditions)


def plan(rows_count, cols_count, tile_rows, tile_cols):
    need = [min(tile_cols, (rows_count * (a + 1) - 1) // cols_count + 1) for a in range(tile_rows)]
    return need, [(a, b) for a in range(tile_rows) for b in range(1, need[a])]


def kernel(
    rows_count, cols_count,
    matrix, checksum, flag,
    work_out, totals_out,
    own, totals, work, new_totals,
    flags, gathered, panel, lead, factor, inverses, inv_tile, cross, sums,
    left_in, right_in, left_out, right_out, low_high, low_low, front, column,
    load_sem, load_totals_sem, load_front_sem, store_sem, store_totals_sem,
    flag_send, flag_recv, gather_send, gather_recv, scan_send, scan_recv, cast_send, cast_recv,
):
    tile_rows, tile_cols, width, _ = totals.shape
    p, q = lax.axis_index("row"), lax.axis_index("col")
    last = cols_count - 1
    bits = rows_count.bit_length() - 1
    need, tiles = plan(rows_count, cols_count, tile_rows, tile_cols)
    ratio = rows_count // cols_count
    wide = PANELS * width
    places = [(a, b) for a in range(tile_rows) for b in range(need[a])]

    def load_front(a):
        return pltpu.make_async_copy(matrix.at[a, :, 0, 0, :], gathered.at[q, a], load_front_sem.at[a])

    def load_totals(a):
        return pltpu.make_async_copy(checksum.at[a], totals.at[a], load_totals_sem.at[a])

    def load_own(t):
        a, b = tiles[t]
        return pltpu.make_async_copy(matrix.at[a, :, b, 0, :], own.at[t], load_sem.at[t])

    def store_totals(b):
        return pltpu.make_async_copy(new_totals.at[b], totals_out.at[b], store_totals_sem.at[b])

    def store_work(i):
        return pltpu.make_async_copy(work.at[i], work_out.at[i], store_sem.at[i])

    load_front(0).start()
    load_totals(0).start()
    for a in range(1, tile_rows):
        load_front(a).start()
        load_totals(a).start()
    for t in range(len(tiles)):
        load_own(t).start()

    barrier = pltpu.get_barrier_semaphore()
    for o in range(cols_count):
        @pl.when(q != o)
        def _():
            pl.semaphore_signal(barrier, inc=1, device_id=(p, jnp.int32(o)), device_id_type=MESH)
    partners = [p + (1 - 2 * bit(p, b)) * (2**b) for b in range(bits)]
    for partner in partners:
        pl.semaphore_signal(barrier, inc=1, device_id=(partner, q), device_id_type=MESH)
    pl.semaphore_wait(barrier, cols_count - 1 + bits)

    def remote(src, dst, send, recv, to):
        return pltpu.make_async_remote_copy(
            src_ref=src, dst_ref=dst, send_sem=send, recv_sem=recv, device_id=to, device_id_type=MESH
        )

    def flag_copy(o):
        return remote(flag, flags, flag_send.at[o], flag_recv, (p, jnp.int32(o)))

    def flag_start():
        @pl.when(q == 0)
        def _():
            for o in range(1, cols_count):
                flag_copy(o).start()
            flags[...] = flag[...]

    def flag_wait():
        @pl.when(q != 0)
        def _():
            flag_copy(0).wait_recv()

    def lost_is(index, shape):
        return jnp.broadcast_to(flags[0:1, 0:1], shape) == index

    sides = (0, 1)
    ahead = [jnp.minimum(q + 1, last), jnp.maximum(q - 1, 0)]

    def gather_copy(side, step, a, origin):
        at = gathered.at[origin, a]
        return remote(at, at, gather_send.at[side, step, a], gather_recv.at[side, step, a], (p, ahead[side]))

    def gather_sends(side, step):
        if side == 0:
            return jnp.logical_and(q - step >= 0, q < last), jnp.maximum(q - step, 0)
        return jnp.logical_and(q + step <= last, q > 0), jnp.minimum(q + step, last)

    def gather_gets(side, step):
        if side == 0:
            return q - 1 - step >= 0, jnp.maximum(q - 1 - step, 0)
        return q + 1 + step <= last, jnp.minimum(q + 1 + step, last)

    def gather_start(step, a):
        for side in sides:
            does, origin = gather_sends(side, step)
            @pl.when(does)
            def _():
                gather_copy(side, step, a, origin).start()

    def gather_wait(step, a):
        for side in sides:
            does, origin = gather_gets(side, step)
            @pl.when(does)
            def _():
                gather_copy(side, step, a, origin).wait_recv()

    def rebuild_panel(a):
        shape = (width, width)
        others = jnp.zeros(shape, F32)
        for o in range(cols_count):
            others = others + jnp.where(lost_is(o, shape), 0.0, gathered[o, a])
        patch = totals[a, 0] - others
        for k in range(PANELS):
            panel[a, :, k * width : (k + 1) * width] = jnp.where(lost_is(k, shape), patch, gathered[k, a])
        front[a] = jnp.where(lost_is(q, shape), patch, gathered[q, a])

    forth = [b for b in range(1, bits)] + [0]
    back = [b for b in range(bits - 1, 0, -1)] + [0]

    class Cast:
        def __init__(self, number, buffer, source, order):
            self.number, self.buffer, self.order = number, buffer, order
            self.apart = [lax.rem(bit(p, b) + bit(source, b), 2) for b in range(bits)]
            self.is_source = p == source

        def copy(self, t):
            return remote(
                self.buffer, self.buffer, cast_send.at[self.number, t], cast_recv.at[self.number],
                (partners[self.order[t]], q),
            )

        def holds(self, t):
            return all_of([self.apart[b] == 0 for b in self.order[t:]])

        def gets(self, t):
            return all_of(
                [self.apart[self.order[t]] == 1] + [self.apart[b] == 0 for b in self.order[t + 1 :]]
            )

        def start(self, t):
            @pl.when(self.holds(t))
            def _():
                self.copy(t).start()

        def wait(self, t):
            @pl.when(self.gets(t))
            def _():
                self.copy(t).wait_recv()

        def finish(self):
            for t in range(bits):
                @pl.when(self.holds(t))
                def _():
                    self.copy(t).wait_send()

    number = iter(range(64))
    def lead_cast(i, k):
        at = lead.at[i * width : (i + 1) * width, k * width : (k + 1) * width]
        return Cast(next(number), at, jnp.int32(i), forth if k else back)

    lead_first = [lead_cast(i, 0) for i in range(PANELS)]
    lead_later = [lead_cast(i, k) for k in range(1, PANELS) for i in range(k, PANELS)]
    orders = (forth, back)
    half = width // 2
    sum_casts = [
        Cast(next(number), sums.at[k * width + h * half : k * width + (h + 1) * half], jnp.int32(k), orders[h])
        for k in range(PANELS)
        for h in range(2)
    ]
    cross_casts = [
        Cast(next(number), cross.at[m, :, h * half : (h + 1) * half], q + cols_count * m, orders[h])
        for m in range(ratio)
        for h in range(2)
    ]

    def cast_start(casts, t):
        for cast in casts:
            cast.start(t)

    def cast_wait(casts, t):
        for cast in casts:
            cast.wait(t)

    def lead_stage():
        for i, cast in enumerate(lead_first):
            @pl.when(cast.is_source)
            def _():
                top = slice(0, (i + 1) * width)
                lead[i * width : (i + 1) * width, top] = panel[0, :, top]

    def sum_stage():
        for k, cast in enumerate(sum_casts[::2]):
            @pl.when(cast.is_source)
            def _():
                for b in range(tile_cols):
                    sums[k * width : (k + 1) * width, b * width : (b + 1) * width] = totals[0, b]

    def cross_stage():
        for m, cast in enumerate(cross_casts[::2]):
            @pl.when(cast.is_source)
            def _():
                for a in range(tile_rows):
                    cross[m, a] = panel[a]

    scan_in, scan_out = (left_in, right_in), (left_out, right_out)
    scan_ends = (0, last)

    count = len(tiles)
    lag = 2
    hops = (q, last - q)

    def scan_copy(side, t, src):
        return remote(src, scan_in[side].at[t], scan_send.at[side, t], scan_recv.at[side, t], (p, ahead[side]))

    def scan_tick(n):
        for side in sides:
            hop = hops[side]
            t = n - lag * hop
            busy = jnp.logical_and(jnp.logical_and(t >= 0, t < count), hop < last)
            t = jnp.clip(t, 0, count - 1)

            @pl.when(jnp.logical_and(busy, hop == 0))
            def _():
                scan_copy(side, t, own.at[t]).start()

            @pl.when(jnp.logical_and(busy, hop > 0))
            def _():
                copy = scan_copy(side, t, scan_out[side].at[t])
                copy.wait_recv()
                scan_out[side][t] = scan_in[side][t] + own[t]
                copy.start()

    def scan_last(t):
        for side in sides:
            @pl.when(q == scan_ends[1 - side])
            def _():
                scan_copy(side, t, scan_out[side].at[t]).wait_recv()
            @pl.when(q == scan_ends[side])
            def _():
                scan_in[side][t] = jnp.zeros((width, width), F32)

    def finish():
        @pl.when(q == 0)
        def _():
            for o in range(1, cols_count):
                flag_copy(o).wait_send()
        for step in range(last):
            for a in range(tile_rows):
                for side in sides:
                    does, origin = gather_sends(side, step)
                    @pl.when(does)
                    def _():
                        gather_copy(side, step, a, origin).wait_send()
        for t in range(len(tiles)):
            for side in sides:
                @pl.when(q != scan_ends[1 - side])
                def _():
                    scan_copy(side, t, scan_out[side].at[t]).wait_send()
        for cast in lead_first + lead_later + sum_casts + cross_casts:
            cast.finish()

    factor[...] = jnp.zeros_like(factor)
    rest = range(1, tile_rows)
    flag_start()
    load_front(0).wait()
    gather_start(0, 0)
    load_totals(0).wait()
    sum_stage()
    cast_start(sum_casts, 0)
    for step in range(last):
        gather_wait(step, 0)
        if step + 1 < last:
            gather_start(step + 1, 0)
        if step + 2 == last:
            for a in rest:
                load_front(a).wait()
                gather_start(0, a)
    flag_wait()
    rebuild_panel(0)
    lead_stage()
    cast_start(lead_first + lead_later, 0)
    for t in range(count):
        load_own(t).wait()
    scan_tick(0)

    def cast_step(casts, t):
        cast_wait(casts, t)
        if t + 1 < bits:
            cast_start(casts, t + 1)

    def gather_step(step):
        for a in rest:
            gather_wait(step, a)
            if step + 1 < last:
                gather_start(step + 1, a)

    for t in range(bits - 1):
        cast_step(lead_first, t)
        cast_step(lead_later, t)
        if t == 0:
            cast_step(sum_casts, 0)
        if t < min(2, last):
            gather_step(t)
    cast_wait(lead_first, bits - 1)

    def cross_begin():
        for a in rest:
            load_totals(a).wait()
            rebuild_panel(a)
        cross_stage()
        cast_start(cross_casts, 0)

    blocks = wide // BLOCK
    service = [[] for _ in range(2 * blocks)]
    service[1] = [lambda step=step: gather_step(step) for step in range(min(bits - 1, 2, last), last)] + [cross_begin]
    service[4] = [lambda: cast_step(sum_casts, 1)]
    service[6] = [lambda: cast_step(cross_casts, 0)]
    service[4] = [lambda: cast_wait(lead_later, bits - 1)] + service[4]
    first_tick = -1

    def serve(n, at):
        for point in range(at, 2 * blocks, 2):
            if service[point]:
                @pl.when(2 * n + at == point)
                def _():
                    for action in service[point]:
                        action()
        scan_tick(2 * n + at - first_tick)

    def column_update(k):
        low, high = k * width, (k + 1) * width
        value = lead[low:, low:high]
        if k:
            value = value - exact_dot(factor[low:, :low], factor[low:high, :low], 1, 1)
        column[low:, :] = value

    def below_update(n, lower, inverse):
        low, high = n * BLOCK, (n + 1) * BLOCK
        at = n % 2 * BLOCK
        factor[low:high, low:high] = lower
        if high < wide:
            below = exact_dot(column[high:, at : at + BLOCK], inverse, 1, 1)
            factor[high:, low:high] = below
            if n % 2 == 0:
                column[high:, BLOCK:] = column[high:, BLOCK:] - exact_dot(below, below[:BLOCK], 1, 1)

    def factor_step(n, carry):
        serve(n, 0)
        for k in range(PANELS):
            @pl.when(n == 2 * k)
            def _():
                column_update(k)
        o = pl.multiple_of(n * BLOCK, BLOCK)
        at = pl.multiple_of(lax.rem(n, 2) * BLOCK, BLOCK)
        lower, inverse = factor_block(column[pl.ds(o, BLOCK), pl.ds(at, BLOCK)], lambda: serve(n, 1))
        inverses[n] = inverse
        for block in range(blocks):
            @pl.when(n == block)
            def _():
                below_update(block, lower, inverse)
        return carry

    lax.fori_loop(0, blocks, factor_step, 0)

    for k in range(PANELS):
        one, two = inverses[2 * k], inverses[2 * k + 1]
        corner = factor[k * width + BLOCK : (k + 1) * width, k * width : k * width + BLOCK]
        inv_tile[k, :BLOCK, :BLOCK] = one
        inv_tile[k, :BLOCK, BLOCK:] = jnp.zeros((BLOCK, BLOCK), F32)
        inv_tile[k, BLOCK:, :BLOCK] = -exact_dot(two, exact_dot(corner, one, 1, 0), 1, 0)
        inv_tile[k, BLOCK:, BLOCK:] = two

    def part(i, m):
        return split(factor[i * width : (i + 1) * width, m * width : (m + 1) * width])

    def solve_rows(x):
        solved = []
        for k in range(PANELS):
            y = x[:, k * width : (k + 1) * width]
            for m in range(k):
                y = y - dot3(split(solved[m]), part(k, m), 1, 1)
            solved.append(dot3(split(y), split(inv_tile[k]), 1, 1))
        return jnp.concatenate(solved, axis=1)

    row_tile = [p + a * rows_count for a in range(tile_rows)]

    def rows_body(a, carry):
        scan_tick(tick + a)
        x = solve_rows(panel[a])
        take = jnp.logical_and(a == 0, p < PANELS)
        top = factor[pl.ds(pl.multiple_of(jnp.minimum(p, PANELS - 1) * width, width), width), :]
        pick = jnp.broadcast_to(jnp.where(take, 1, 0), x.shape) == 1
        x = jnp.where(pick, top, x)
        panel[a] = x
        low_high[a], low_low[a] = split(x)
        return carry

    tick = 2 * blocks - first_tick
    lax.fori_loop(0, tile_rows, rows_body, 0)
    tick += tile_rows

    for t in range(2, bits):
        cast_step(sum_casts, t)
    cast_step(cross_casts, 1)

    def sums_body(b, carry):
        scan_tick(tick + b)
        at = pl.ds(pl.multiple_of(b * width, width), width)
        solved = []
        for k in range(PANELS):
            y = sums[k * width : (k + 1) * width, at]
            for m in range(k):
                y = y - dot3(part(k, m), solved[m], 1, 0)
            solved.append(split(dot3(split(inv_tile[k]), split(y), 1, 0)))
        y = (jnp.concatenate([s[0] for s in solved], 0), jnp.concatenate([s[1] for s in solved], 0))
        for a in range(tile_rows):
            new_totals[b, a] = totals[a, b] - dot3((low_high[a], low_low[a]), y, 1, 0)
        store_totals(b).start()
        return carry

    lax.fori_loop(0, tile_cols, sums_body, 0)
    tick += tile_cols
    for t in range(2, bits):
        cast_step(cross_casts, t)

    for b in range(tile_cols):
        scan_tick(tick + b)
        y = split(solve_rows(cross[b % ratio, b // ratio]))
        for a in range(tile_rows):
            if b < need[a]:
                work[places.index((a, b))] = dot3((low_high[a], low_low[a]), y, 1, 1)
    tick += tile_cols
    ticks = count + lag * (last - 1)

    def tick_body(n, carry):
        scan_tick(n)
        return carry

    if ticks > tick:
        lax.fori_loop(tick, ticks, tick_body, 0)
    for t in range(count):
        scan_last(t)

    shape = (width, width)
    for i, (a, b) in enumerate(places):
        if b == 0:
            value = front[a] - work[i]
            for k in range(PANELS):
                value = jnp.where(
                    jnp.broadcast_to(q, shape) == k, panel[a, :, k * width : (k + 1) * width], value
                )
        else:
            t = tiles.index((a, b))
            back_in = totals[a, b] - (left_in[t] + right_in[t])
            value = jnp.where(lost_is(q, shape), back_in, own[t]) - work[i]
        keep = jnp.broadcast_to(row_tile[a], shape) >= jnp.broadcast_to(q + b * cols_count, shape)
        work[i] = jnp.where(keep, value, 0.0)
        store_work(i).start()
    for i in range(len(places)):
        store_work(i).wait()
    for b in range(tile_cols):
        store_totals(b).wait()
    finish()


def place_kernel(places, work, totals, work_out, totals_out, held, zero, held_totals, load, store, load_t, store_t):
    cols, rows = totals.shape[:2]
    loads = [pltpu.make_async_copy(work.at[i], held.at[i], load.at[i]) for i in range(len(places))]
    loads_t = [pltpu.make_async_copy(totals.at[b], held_totals.at[b], load_t.at[b]) for b in range(cols)]
    for copy in loads + loads_t:
        copy.start()
    zero[...] = jnp.zeros_like(zero)
    stores = []
    for a in range(rows):
        for b in range(cols):
            to = work_out.at[a, :, b, 0, :]
            if (a, b) not in places:
                stores.append(pltpu.make_async_copy(zero, to, store.at[a, b]))
                stores[-1].start()
    for i, (a, b) in enumerate(places):
        loads[i].wait()
        stores.append(pltpu.make_async_copy(held.at[i], work_out.at[a, :, b, 0, :], store.at[a, b]))
        stores[-1].start()
    for b in range(cols):
        loads_t[b].wait()
        for a in range(rows):
            stores.append(pltpu.make_async_copy(held_totals.at[b, a], totals_out.at[a, b], store_t.at[a, b]))
            stores[-1].start()
    for copy in stores:
        copy.wait()


def shards(matrix, checksum, failed):
    rows_count, cols_count = lax.axis_size("row"), lax.axis_size("col")
    tile_rows, width, tile_cols = matrix.shape[1], matrix.shape[2], matrix.shape[4]
    assert width == 2 * BLOCK and rows_count % cols_count == 0
    assert cols_count >= PANELS and rows_count & (rows_count - 1) == 0
    own = matrix.reshape(tile_rows, width, tile_cols, 1, width)
    totals = checksum.reshape(tile_rows, width, tile_cols, width).transpose(0, 2, 1, 3)
    flag = jnp.broadcast_to(failed.reshape(1, 1), (8, 128))
    wide = PANELS * width
    bits = rows_count.bit_length() - 1
    ratio = rows_count // cols_count
    need, tiles = plan(rows_count, cols_count, tile_rows, tile_cols)
    count = len(tiles)
    casts = PANELS * (PANELS + 1) // 2 + 2 * PANELS + 2 * ratio
    vmem = pl.BlockSpec(memory_space=pltpu.VMEM)
    dma = pltpu.SemaphoreType.DMA
    hbm = pl.BlockSpec(memory_space=pl.ANY)
    places = [(a, b) for a in range(tile_rows) for b in range(need[a])]
    tile = lambda *n: pltpu.VMEM((*n, width, width), F32)
    shape = lambda *n: jax.ShapeDtypeStruct((*n, width, width), F32)
    work, new_totals = pl.pallas_call(
        functools.partial(kernel, rows_count, cols_count),
        out_shape=[shape(len(places)), shape(tile_cols, tile_rows)],
        in_specs=[hbm, hbm, vmem],
        out_specs=[hbm, hbm],
        scratch_shapes=[
            tile(count),
            tile(tile_rows, tile_cols),
            tile(len(places)),
            tile(tile_cols, tile_rows),
            pltpu.VMEM((8, 128), jnp.int32),
            pltpu.VMEM((cols_count, tile_rows, width, width), F32),
            pltpu.VMEM((tile_rows, width, wide), F32),
            pltpu.VMEM((wide, wide), F32),
            pltpu.VMEM((wide, wide), F32),
            pltpu.VMEM((wide // BLOCK, BLOCK, BLOCK), F32),
            pltpu.VMEM((PANELS, width, width), F32),
            pltpu.VMEM((ratio, tile_rows, width, wide), F32),
            pltpu.VMEM((wide, tile_cols * width), F32),
        ]
        + [pltpu.VMEM((count, width, width), F32)] * 4
        + [pltpu.VMEM((tile_rows, width, wide), BF16)] * 2
        + [pltpu.VMEM((tile_rows, width, width), F32), pltpu.VMEM((wide, width), F32)]
        + [
            dma((count,)),
            dma((tile_rows,)),
            dma((tile_rows,)),
            dma((len(places),)),
            dma((tile_cols,)),
            dma((cols_count,)),
            dma,
            dma((2, cols_count - 1, tile_rows)),
            dma((2, cols_count - 1, tile_rows)),
            dma((2, count)),
            dma((2, count)),
            dma((casts, bits)),
            dma((casts,)),
        ],
        compiler_params=pltpu.CompilerParams(
            collective_id=0, has_side_effects=True, vmem_limit_bytes=62 * 2**20
        ),
        cost_estimate=pl.CostEstimate(flops=30 * 10**9, bytes_accessed=20 * 10**6, transcendentals=0),
    )(own, totals, flag)
    work, new_totals = pl.pallas_call(
        functools.partial(place_kernel, places),
        out_shape=[jax.ShapeDtypeStruct(own.shape, F32), shape(tile_rows, tile_cols)],
        in_specs=[hbm, hbm],
        out_specs=[hbm, hbm],
        scratch_shapes=[
            tile(len(places)),
            tile(),
            tile(tile_cols, tile_rows),
            dma((len(places),)),
            dma((tile_rows, tile_cols)),
            dma((tile_cols,)),
            dma((tile_rows, tile_cols)),
        ],
        compiler_params=pltpu.CompilerParams(vmem_limit_bytes=62 * 2**20),
        cost_estimate=pl.CostEstimate(flops=0, bytes_accessed=20 * 10**6, transcendentals=0),
    )(work, new_totals)
    new_totals = new_totals.transpose(0, 2, 1, 3)
    return work.reshape(matrix.shape), new_totals.reshape(checksum.shape)


def solution(mesh):
    return jax.shard_map(
        shards,
        mesh=mesh,
        in_specs=(
            P("row", None, None, "col", None, None),
            P("row", None, None, None, None),
            P("col"),
        ),
        out_specs=(P("row", None, None, "col", None, None), P("row", None, None, None, None)),
        check_vma=False,
    )
```

```python
import functools

import jax
import jax.numpy as jnp
from jax import lax
from jax.experimental import pallas as pl
from jax.experimental.pallas import tpu as pltpu
from jax.sharding import PartitionSpec as P

PANELS = 3
BLOCK = 128
EXACT = lax.Precision.HIGHEST
MESH = pl.DeviceIdType.MESH
F32 = jnp.float32
BF16 = jnp.bfloat16


def exact_dot(a, b, ca, cb):
    return lax.dot_general(
        a, b, (((ca,), (cb,)), ((), ())), precision=EXACT, preferred_element_type=F32
    )


def split(x):
    high = x.astype(BF16)
    return high, (x - high.astype(F32)).astype(BF16)


def dot3(a, b, ca, cb):
    dims = (((ca,), (cb,)), ((), ()))
    make = lambda x, y: lax.dot_general(x, y, dims, preferred_element_type=F32)
    return make(a[0], b[0]) + (make(a[0], b[1]) + make(a[1], b[0]))


def factor_block(block, middle):
    n = block.shape[0]
    groups = n // 8
    rows = lax.broadcasted_iota(jnp.int32, (8, n), 0)
    lanes = lax.broadcasted_iota(jnp.int32, (8, n), 1)
    a = [block[8 * h : 8 * h + 8, :] for h in range(groups)]
    m = [jnp.where(lanes == rows + 8 * h, 1.0, 0.0).astype(F32) for h in range(groups)]
    lane = lambda x, j: jnp.broadcast_to(x[:, j : j + 1], (8, n))
    row = lambda x, j: jnp.broadcast_to(x[j : j + 1, :], (8, n))
    for g in range(groups):
        if g == groups // 2:
            middle()
        cols = [[lane(a[h], 8 * g + l) for l in range(8)] for h in range(g, groups)]
        for j in range(8):
            scale = lax.rsqrt(row(cols[0][j], j))
            a_row = row(a[g], j) * scale
            m_row = row(m[g], j) * scale
            heads = [row(cols[0][l], j) * scale for l in range(j + 1, 8)]
            for h in range(g, groups):
                c = cols[h - g][j] * scale
                if h == g:
                    below = jnp.where(rows > j, c, 0.0)
                    a[h] = jnp.where(rows == j, a_row, a[h] - below * a_row)
                    m[h] = jnp.where(rows == j, m_row, m[h] - below * m_row)
                else:
                    a[h] = a[h] - c * a_row
                    m[h] = m[h] - c * m_row
                for l in range(j + 1, 8):
                    cols[h - g][l] = cols[h - g][l] - c * heads[l - j - 1]
    upper = jnp.concatenate(a, axis=0)
    inverse = jnp.concatenate(m, axis=0)
    r = lax.broadcasted_iota(jnp.int32, (n, n), 0)
    c = lax.broadcasted_iota(jnp.int32, (n, n), 1)
    return jnp.where(r <= c, upper, 0.0).T, jnp.where(r >= c, inverse, 0.0)


def bit(value, b):
    return lax.rem(value // (2**b), 2)


def all_of(conditions):
    return functools.reduce(jnp.logical_and, conditions)


def plan(rows_count, cols_count, tile_rows, tile_cols):
    need = [min(tile_cols, (rows_count * (a + 1) - 1) // cols_count + 1) for a in range(tile_rows)]
    return need, [(a, b) for a in range(tile_rows) for b in range(1, need[a])]


def kernel(
    rows_count, cols_count,
    matrix, checksum, flag,
    work_out, totals_out,
    own, totals, work, new_totals,
    flags, gathered, panel, lead, factor, inverses, inv_tile, cross, sums,
    left_in, right_in, left_out, right_out, low_high, low_low, front, column,
    load_sem, load_totals_sem, load_front_sem, store_sem, store_totals_sem,
    flag_send, flag_recv, gather_send, gather_recv, scan_send, scan_recv, cast_send, cast_recv,
):
    tile_rows, tile_cols, width, _ = totals.shape
    p, q = lax.axis_index("row"), lax.axis_index("col")
    last = cols_count - 1
    bits = rows_count.bit_length() - 1
    need, tiles = plan(rows_count, cols_count, tile_rows, tile_cols)
    ratio = rows_count // cols_count
    wide = PANELS * width
    places = [(a, b) for a in range(tile_rows) for b in range(need[a])]

    def load_front(a):
        return pltpu.make_async_copy(matrix.at[a, :, 0, 0, :], gathered.at[q, a], load_front_sem.at[a])

    def load_totals(a):
        return pltpu.make_async_copy(checksum.at[a], totals.at[a], load_totals_sem.at[a])

    def load_own(t):
        a, b = tiles[t]
        return pltpu.make_async_copy(matrix.at[a, :, b, 0, :], own.at[t], load_sem.at[t])

    def store_totals(b):
        return pltpu.make_async_copy(new_totals.at[b], totals_out.at[b], store_totals_sem.at[b])

    def store_work(i):
        return pltpu.make_async_copy(work.at[i], work_out.at[i], store_sem.at[i])

    load_front(0).start()
    load_totals(0).start()
    for a in range(1, tile_rows):
        load_front(a).start()
        load_totals(a).start()
    for t in range(len(tiles)):
        load_own(t).start()

    barrier = pltpu.get_barrier_semaphore()
    for o in range(cols_count):
        @pl.when(q != o)
        def _():
            pl.semaphore_signal(barrier, inc=1, device_id=(p, jnp.int32(o)), device_id_type=MESH)
    partners = [p + (1 - 2 * bit(p, b)) * (2**b) for b in range(bits)]
    for partner in partners:
        pl.semaphore_signal(barrier, inc=1, device_id=(partner, q), device_id_type=MESH)
    pl.semaphore_wait(barrier, cols_count - 1 + bits)

    def remote(src, dst, send, recv, to):
        return pltpu.make_async_remote_copy(
            src_ref=src, dst_ref=dst, send_sem=send, recv_sem=recv, device_id=to, device_id_type=MESH
        )

    def flag_copy(o):
        return remote(flag, flags, flag_send.at[o], flag_recv, (p, jnp.int32(o)))

    def flag_start():
        @pl.when(q == 0)
        def _():
            for o in range(1, cols_count):
                flag_copy(o).start()
            flags[...] = flag[...]

    def flag_wait():
        @pl.when(q != 0)
        def _():
            flag_copy(0).wait_recv()

    def lost_is(index, shape):
        return jnp.broadcast_to(flags[0:1, 0:1], shape) == index

    sides = (0, 1)
    ahead = [jnp.minimum(q + 1, last), jnp.maximum(q - 1, 0)]

    def gather_copy(side, step, a, origin):
        at = gathered.at[origin, a]
        return remote(at, at, gather_send.at[side, step, a], gather_recv.at[side, step, a], (p, ahead[side]))

    def gather_sends(side, step):
        if side == 0:
            return jnp.logical_and(q - step >= 0, q < last), jnp.maximum(q - step, 0)
        return jnp.logical_and(q + step <= last, q > 0), jnp.minimum(q + step, last)

    def gather_gets(side, step):
        if side == 0:
            return q - 1 - step >= 0, jnp.maximum(q - 1 - step, 0)
        return q + 1 + step <= last, jnp.minimum(q + 1 + step, last)

    def gather_start(step, a):
        for side in sides:
            does, origin = gather_sends(side, step)
            @pl.when(does)
            def _():
                gather_copy(side, step, a, origin).start()

    def gather_wait(step, a):
        for side in sides:
            does, origin = gather_gets(side, step)
            @pl.when(does)
            def _():
                gather_copy(side, step, a, origin).wait_recv()

    def rebuild_panel(a):
        shape = (width, width)
        others = jnp.zeros(shape, F32)
        for o in range(cols_count):
            others = others + jnp.where(lost_is(o, shape), 0.0, gathered[o, a])
        patch = totals[a, 0] - others
        for k in range(PANELS):
            panel[a, :, k * width : (k + 1) * width] = jnp.where(lost_is(k, shape), patch, gathered[k, a])
        front[a] = jnp.where(lost_is(q, shape), patch, gathered[q, a])

    forth = [b for b in range(1, bits)] + [0]
    back = [b for b in range(bits - 1, 0, -1)] + [0]

    class Cast:
        def __init__(self, number, buffer, source, order):
            self.number, self.buffer, self.order = number, buffer, order
            self.apart = [lax.rem(bit(p, b) + bit(source, b), 2) for b in range(bits)]
            self.is_source = p == source

        def copy(self, t):
            return remote(
                self.buffer, self.buffer, cast_send.at[self.number, t], cast_recv.at[self.number],
                (partners[self.order[t]], q),
            )

        def holds(self, t):
            return all_of([self.apart[b] == 0 for b in self.order[t:]])

        def gets(self, t):
            return all_of(
                [self.apart[self.order[t]] == 1] + [self.apart[b] == 0 for b in self.order[t + 1 :]]
            )

        def start(self, t):
            @pl.when(self.holds(t))
            def _():
                self.copy(t).start()

        def wait(self, t):
            @pl.when(self.gets(t))
            def _():
                self.copy(t).wait_recv()

        def finish(self):
            for t in range(bits):
                @pl.when(self.holds(t))
                def _():
                    self.copy(t).wait_send()

    number = iter(range(99))
    def lead_cast(i, k):
        at = lead.at[i * width : (i + 1) * width, k * width : (k + 1) * width]
        return Cast(next(number), at, jnp.int32(i), forth if k else back)

    lead_first = [lead_cast(i, 0) for i in range(PANELS)]
    lead_later = [lead_cast(i, k) for k in range(1, PANELS) for i in range(k, PANELS)]
    orders = (forth, back)
    half = width // 2
    sum_casts = [
        Cast(next(number), sums.at[k * width + h * half : k * width + (h + 1) * half], jnp.int32(k), orders[h])
        for k in range(PANELS)
        for h in range(2)
    ]
    cross_casts = [
        [
            Cast(next(number), cross.at[m, a, h * half : (h + 1) * half], q + cols_count * m, orders[h])
            for m in range(ratio)
            for h in range(2)
        ]
        for a in range(tile_rows)
    ]

    def cast_start(casts, t):
        for cast in casts:
            cast.start(t)

    def cast_wait(casts, t):
        for cast in casts:
            cast.wait(t)

    def lead_stage():
        for i, cast in enumerate(lead_first):
            @pl.when(cast.is_source)
            def _():
                top = slice(0, (i + 1) * width)
                lead[i * width : (i + 1) * width, top] = panel[0, :, top]

    def sum_stage():
        for k, cast in enumerate(sum_casts[::2]):
            @pl.when(cast.is_source)
            def _():
                for b in range(tile_cols):
                    sums[k * width : (k + 1) * width, b * width : (b + 1) * width] = totals[0, b]

    def cross_begin(a):
        for m, cast in enumerate(cross_casts[a][::2]):
            @pl.when(cast.is_source)
            def _():
                cross[m, a] = panel[a]
        cast_start(cross_casts[a], 0)

    scan_in, scan_out = (left_in, right_in), (left_out, right_out)
    scan_ends = (0, last)

    count = len(tiles)
    lag = 2
    hops = (q, last - q)

    def scan_copy(side, t, src):
        return remote(src, scan_in[side].at[t], scan_send.at[side, t], scan_recv.at[side, t], (p, ahead[side]))

    def scan_below(t):
        off = jnp.int32(0)
        for i, (a, b) in enumerate(tiles):
            off = jnp.where(t == i, rows_count * a - cols_count * b, off)
        return p + off

    def scan_gets(side, t):
        return jnp.logical_and(hops[side] > 0, scan_below(t) >= (0 if side else q))

    def scan_sends(side, t):
        return jnp.logical_and(hops[side] < last, scan_below(t) >= (0 if side else q + 1))

    def scan_tick(n):
        for side in sides:
            hop = hops[side]
            t = n - lag * hop
            busy = jnp.logical_and(t >= 0, t < count)
            t = jnp.clip(t, 0, count - 1)
            busy = jnp.logical_and(busy, scan_sends(side, t))

            @pl.when(jnp.logical_and(busy, hop == 0))
            def _():
                scan_copy(side, t, own.at[t]).start()

            @pl.when(jnp.logical_and(busy, hop > 0))
            def _():
                copy = scan_copy(side, t, scan_out[side].at[t])
                copy.wait_recv()
                scan_out[side][t] = scan_in[side][t] + own[t]
                copy.start()

    def scan_last(t):
        for side in sides:
            @pl.when(jnp.logical_and(scan_gets(side, t), jnp.logical_not(scan_sends(side, t))))
            def _():
                scan_copy(side, t, scan_out[side].at[t]).wait_recv()
            @pl.when(q == scan_ends[side])
            def _():
                scan_in[side][t] = jnp.zeros((width, width), F32)

    def finish():
        @pl.when(q == 0)
        def _():
            for o in range(1, cols_count):
                flag_copy(o).wait_send()
        for step in range(last):
            for a in range(tile_rows):
                for side in sides:
                    does, origin = gather_sends(side, step)
                    @pl.when(does)
                    def _():
                        gather_copy(side, step, a, origin).wait_send()
        for t in range(len(tiles)):
            for side in sides:
                @pl.when(scan_sends(side, t))
                def _():
                    scan_copy(side, t, scan_out[side].at[t]).wait_send()
        for cast in lead_first + lead_later + sum_casts + sum(cross_casts, []):
            cast.finish()

    factor[...] = jnp.zeros_like(factor)
    rest = range(1, tile_rows)
    flag_start()
    load_front(0).wait()
    gather_start(0, 0)
    load_totals(0).wait()
    sum_stage()
    cast_start(sum_casts, 0)
    def rest_start():
        for a in rest:
            gather_start(0, a)

    for step in range(last):
        gather_wait(step, 0)
        if step + 1 < last:
            gather_start(step + 1, 0)
        if step == 0:
            for a in rest:
                load_front(a).wait()

            @pl.when(p > PANELS)
            def _():
                rest_start()


    @pl.when(p <= PANELS)
    def _():
        rest_start()

    flag_wait()
    rebuild_panel(0)
    lead_stage()
    cast_start(lead_first + lead_later, 0)
    for t in range(count):
        load_own(t).wait()
    scan_tick(0)

    def cast_step(casts, t):
        cast_wait(casts, t)
        if t + 1 < bits:
            cast_start(casts, t + 1)

    def gather_step(step):
        for a in rest:
            gather_wait(step, a)
            if step + 1 < last:
                gather_start(step + 1, a)

    for t in range(bits - 1):
        cast_step(lead_first, t)
        cast_step(lead_later, t)
    cast_wait(lead_first, bits - 1)
    cast_step(sum_casts, 0)
    cross_begin(0)

    def panel_ready(a):
        load_totals(a).wait()
        rebuild_panel(a)
        cross_begin(a)

    blocks = wide // BLOCK
    service = {point: [] for point in range(2 * blocks)}
    service[0] += [lambda: gather_step(0)]
    service[1] += [lambda: gather_step(1)]
    service[2] += [lambda step=step: gather_step(step) for step in range(2, last)]
    service[2] += [lambda a=a: panel_ready(a) for a in rest]
    service[8] += [lambda: cast_step(sum_casts, 1)]
    service[5] += [lambda: cast_step(cross_casts[0], 0)]
    service[8] += [lambda a=a: cast_step(cross_casts[a], 0) for a in rest]
    service[10] += [lambda: cast_step(cross_casts[0], 1)]
    service[4] = [lambda: cast_wait(lead_later, bits - 1)] + service[4]
    ticks_at = (0, 2, 4, 6, 8, 10)
    first_tick = 1

    def serve(n, at):
        for point in range(at, 2 * blocks, 2):
            if service[point]:
                @pl.when(2 * n + at == point)
                def _():
                    for action in service[point]:
                        action()
        done = jnp.int32(first_tick)
        now = jnp.int32(0)
        for point in ticks_at:
            done = done + jnp.where(2 * n + at > point, 1, 0)
            now = now + jnp.where(2 * n + at == point, 1, 0)

        @pl.when(now > 0)
        def _():
            scan_tick(done)


    def column_update(k):
        low, high = k * width, (k + 1) * width
        value = lead[low:, low:high]
        if k:
            value = value - exact_dot(factor[low:, :low], factor[low:high, :low], 1, 1)
        column[low:, :] = value

    def below_update(n, lower, inverse):
        low, high = n * BLOCK, (n + 1) * BLOCK
        at = n % 2 * BLOCK
        factor[low:high, low:high] = lower
        if high < wide:
            below = exact_dot(column[high:, at : at + BLOCK], inverse, 1, 1)
            factor[high:, low:high] = below
            if n % 2 == 0:
                column[high:, BLOCK:] = column[high:, BLOCK:] - exact_dot(below, below[:BLOCK], 1, 1)

    def factor_step(n, carry):
        serve(n, 0)
        for k in range(PANELS):
            @pl.when(n == 2 * k)
            def _():
                column_update(k)
        o = pl.multiple_of(n * BLOCK, BLOCK)
        at = pl.multiple_of(lax.rem(n, 2) * BLOCK, BLOCK)
        lower, inverse = factor_block(column[pl.ds(o, BLOCK), pl.ds(at, BLOCK)], lambda: serve(n, 1))
        inverses[n] = inverse
        for block in range(blocks):
            @pl.when(n == block)
            def _():
                below_update(block, lower, inverse)
        return carry

    lax.fori_loop(0, blocks, factor_step, 0)

    for k in range(PANELS):
        one, two = inverses[2 * k], inverses[2 * k + 1]
        corner = factor[k * width + BLOCK : (k + 1) * width, k * width : k * width + BLOCK]
        inv_tile[k, :BLOCK, :BLOCK] = one
        inv_tile[k, :BLOCK, BLOCK:] = jnp.zeros((BLOCK, BLOCK), F32)
        inv_tile[k, BLOCK:, :BLOCK] = -exact_dot(two, exact_dot(corner, one, 1, 0), 1, 0)
        inv_tile[k, BLOCK:, BLOCK:] = two

    def part(i, m):
        return split(factor[i * width : (i + 1) * width, m * width : (m + 1) * width])

    def solve_rows(x):
        solved = []
        for k in range(PANELS):
            y = x[:, k * width : (k + 1) * width]
            for m in range(k):
                y = y - dot3(split(solved[m]), part(k, m), 1, 1)
            solved.append(dot3(split(y), split(inv_tile[k]), 1, 1))
        return jnp.concatenate(solved, axis=1)

    def serve_later(tick, n, every):
        @pl.when(lax.rem(n, every) == 0)
        def _():
            scan_tick(tick + n // every)

    row_tile = [p + a * rows_count for a in range(tile_rows)]

    def rows_body(a, carry):
        serve_later(tick, a, 2)
        x = solve_rows(panel[a])
        take = jnp.logical_and(a == 0, p < PANELS)
        top = factor[pl.ds(pl.multiple_of(jnp.minimum(p, PANELS - 1) * width, width), width), :]
        pick = jnp.broadcast_to(jnp.where(take, 1, 0), x.shape) == 1
        x = jnp.where(pick, top, x)
        panel[a] = x
        low_high[a], low_low[a] = split(x)
        return carry

    tick = first_tick + len(ticks_at)
    lax.fori_loop(0, tile_rows, rows_body, 0)
    tick += -(-tile_rows // 2)

    for t in range(2, bits):
        cast_step(sum_casts, t)
    for a in rest:
        cast_step(cross_casts[a], 1)

    def sums_body(b, carry):
        serve_later(tick, b, 2)
        at = pl.ds(pl.multiple_of(b * width, width), width)
        solved = []
        for k in range(PANELS):
            y = sums[k * width : (k + 1) * width, at]
            for m in range(k):
                y = y - dot3(part(k, m), solved[m], 1, 0)
            solved.append(split(dot3(split(inv_tile[k]), split(y), 1, 0)))
        y = (jnp.concatenate([s[0] for s in solved], 0), jnp.concatenate([s[1] for s in solved], 0))
        for a in range(tile_rows):
            new_totals[b, a] = totals[a, b] - dot3((low_high[a], low_low[a]), y, 1, 0)
        store_totals(b).start()
        return carry

    lax.fori_loop(0, tile_cols, sums_body, 0)
    tick += -(-tile_cols // 2)

    for b in range(tile_cols):
        if b % 2 == 0:
            scan_tick(tick + b // 2)
        if b % ratio == 0:
            for t in range(2, bits):
                cast_step(cross_casts[b // ratio], t)
        y = split(solve_rows(cross[b % ratio, b // ratio]))
        for a in range(tile_rows):
            if b < need[a]:
                work[places.index((a, b))] = dot3((low_high[a], low_low[a]), y, 1, 1)
    tick += -(-tile_cols // 2)
    ticks = count + lag * (last - 1)

    def tick_body(n, carry):
        scan_tick(n)
        return carry

    if ticks > tick:
        lax.fori_loop(tick, ticks, tick_body, 0)
    shape = (width, width)
    for i, (a, b) in enumerate(places):
        if b == 0:
            value = front[a] - work[i]
            for k in range(PANELS):
                value = jnp.where(
                    jnp.broadcast_to(q, shape) == k, panel[a, :, k * width : (k + 1) * width], value
                )
        else:
            t = tiles.index((a, b))
            scan_last(t)
            back_in = totals[a, b] - (left_in[t] + right_in[t])
            value = jnp.where(lost_is(q, shape), back_in, own[t]) - work[i]
        keep = jnp.broadcast_to(row_tile[a], shape) >= jnp.broadcast_to(q + b * cols_count, shape)
        work[i] = jnp.where(keep, value, 0.0)
        store_work(i).start()
    for i in range(len(places)):
        store_work(i).wait()
    for b in range(tile_cols):
        store_totals(b).wait()
    finish()


def place_kernel(places, work, totals, work_out, totals_out, held, zero, held_totals, load, store, load_t, store_t):
    cols, rows = totals.shape[:2]
    loads = [pltpu.make_async_copy(work.at[i], held.at[i], load.at[i]) for i in range(len(places))]
    loads_t = [pltpu.make_async_copy(totals.at[b], held_totals.at[b], load_t.at[b]) for b in range(cols)]
    for copy in loads + loads_t:
        copy.start()
    zero[...] = jnp.zeros_like(zero)
    stores = []
    for a in range(rows):
        for b in range(cols):
            to = work_out.at[a, :, b, 0, :]
            if (a, b) not in places:
                stores.append(pltpu.make_async_copy(zero, to, store.at[a, b]))
                stores[-1].start()
    for i, (a, b) in enumerate(places):
        loads[i].wait()
        stores.append(pltpu.make_async_copy(held.at[i], work_out.at[a, :, b, 0, :], store.at[a, b]))
        stores[-1].start()
    for b in range(cols):
        loads_t[b].wait()
        for a in range(rows):
            stores.append(pltpu.make_async_copy(held_totals.at[b, a], totals_out.at[a, b], store_t.at[a, b]))
            stores[-1].start()
    for copy in stores:
        copy.wait()


def shards(matrix, checksum, failed):
    rows_count, cols_count = lax.axis_size("row"), lax.axis_size("col")
    tile_rows, width, tile_cols = matrix.shape[1], matrix.shape[2], matrix.shape[4]
    assert width == 2 * BLOCK and rows_count % cols_count == 0
    assert cols_count >= PANELS and rows_count & (rows_count - 1) == 0
    own = matrix.reshape(tile_rows, width, tile_cols, 1, width)
    totals = checksum.reshape(tile_rows, width, tile_cols, width).transpose(0, 2, 1, 3)
    flag = jnp.broadcast_to(failed.reshape(1, 1), (8, 128))
    wide = PANELS * width
    bits = rows_count.bit_length() - 1
    ratio = rows_count // cols_count
    need, tiles = plan(rows_count, cols_count, tile_rows, tile_cols)
    count = len(tiles)
    casts = PANELS * (PANELS + 1) // 2 + 2 * PANELS + 2 * ratio * tile_rows
    vmem = pl.BlockSpec(memory_space=pltpu.VMEM)
    dma = pltpu.SemaphoreType.DMA
    hbm = pl.BlockSpec(memory_space=pl.ANY)
    places = [(a, b) for a in range(tile_rows) for b in range(need[a])]
    tile = lambda *n: pltpu.VMEM((*n, width, width), F32)
    shape = lambda *n: jax.ShapeDtypeStruct((*n, width, width), F32)
    work, new_totals = pl.pallas_call(
        functools.partial(kernel, rows_count, cols_count),
        out_shape=[shape(len(places)), shape(tile_cols, tile_rows)],
        in_specs=[hbm, hbm, vmem],
        out_specs=[hbm, hbm],
        scratch_shapes=[
            tile(count),
            tile(tile_rows, tile_cols),
            tile(len(places)),
            tile(tile_cols, tile_rows),
            pltpu.VMEM((8, 128), jnp.int32),
            pltpu.VMEM((cols_count, tile_rows, width, width), F32),
            pltpu.VMEM((tile_rows, width, wide), F32),
            pltpu.VMEM((wide, wide), F32),
            pltpu.VMEM((wide, wide), F32),
            pltpu.VMEM((wide // BLOCK, BLOCK, BLOCK), F32),
            pltpu.VMEM((PANELS, width, width), F32),
            pltpu.VMEM((ratio, tile_rows, width, wide), F32),
            pltpu.VMEM((wide, tile_cols * width), F32),
        ]
        + [pltpu.VMEM((count, width, width), F32)] * 4
        + [pltpu.VMEM((tile_rows, width, wide), BF16)] * 2
        + [pltpu.VMEM((tile_rows, width, width), F32), pltpu.VMEM((wide, width), F32)]
        + [
            dma((count,)),
            dma((tile_rows,)),
            dma((tile_rows,)),
            dma((len(places),)),
            dma((tile_cols,)),
            dma((cols_count,)),
            dma,
            dma((2, cols_count - 1, tile_rows)),
            dma((2, cols_count - 1, tile_rows)),
            dma((2, count)),
            dma((2, count)),
            dma((casts, bits)),
            dma((casts,)),
        ],
        compiler_params=pltpu.CompilerParams(
            collective_id=0, has_side_effects=True, vmem_limit_bytes=62 * 2**20
        ),
        cost_estimate=pl.CostEstimate(flops=30 * 10**9, bytes_accessed=20 * 10**6, transcendentals=0),
    )(own, totals, flag)
    work, new_totals = pl.pallas_call(
        functools.partial(place_kernel, places),
        out_shape=[jax.ShapeDtypeStruct(own.shape, F32), shape(tile_rows, tile_cols)],
        in_specs=[hbm, hbm],
        out_specs=[hbm, hbm],
        scratch_shapes=[
            tile(len(places)),
            tile(),
            tile(tile_cols, tile_rows),
            dma((len(places),)),
            dma((tile_rows, tile_cols)),
            dma((tile_cols,)),
            dma((tile_rows, tile_cols)),
        ],
        compiler_params=pltpu.CompilerParams(vmem_limit_bytes=62 * 2**20),
        cost_estimate=pl.CostEstimate(flops=0, bytes_accessed=20 * 10**6, transcendentals=0),
    )(work, new_totals)
    new_totals = new_totals.transpose(0, 2, 1, 3)
    return work.reshape(matrix.shape), new_totals.reshape(checksum.shape)


def solution(mesh):
    return jax.shard_map(
        shards,
        mesh=mesh,
        in_specs=(
            P("row", None, None, "col", None, None),
            P("row", None, None, None, None),
            P("col"),
        ),
        out_specs=(P("row", None, None, "col", None, None), P("row", None, None, None, None)),
        check_vma=False,
    )
```

```python
import functools

import jax
import jax.numpy as jnp
from jax import lax
from jax.experimental import pallas as pl
from jax.experimental.pallas import tpu as pltpu
from jax.sharding import PartitionSpec as P

PANELS = 3
BLOCK = 128
EXACT = lax.Precision.HIGHEST
MESH = pl.DeviceIdType.MESH
F32 = jnp.float32
BF16 = jnp.bfloat16


def exact_dot(a, b, ca, cb):
    return lax.dot_general(
        a, b, (((ca,), (cb,)), ((), ())), precision=EXACT, preferred_element_type=F32
    )


def split(x):
    high = x.astype(BF16)
    return high, (x - high.astype(F32)).astype(BF16)


def dot3(a, b, ca, cb):
    dims = (((ca,), (cb,)), ((), ()))
    make = lambda x, y: lax.dot_general(x, y, dims, preferred_element_type=F32)
    return make(a[0], b[0]) + (make(a[0], b[1]) + make(a[1], b[0]))


def factor_block(block, middle):
    n = block.shape[0]
    groups = n // 8
    rows = lax.broadcasted_iota(jnp.int32, (8, n), 0)
    lanes = lax.broadcasted_iota(jnp.int32, (8, n), 1)
    a = [block[8 * h : 8 * h + 8, :] for h in range(groups)]
    m = [jnp.where(lanes == rows + 8 * h, 1.0, 0.0).astype(F32) for h in range(groups)]
    lane = lambda x, j: jnp.broadcast_to(x[:, j : j + 1], (8, n))
    row = lambda x, j: jnp.broadcast_to(x[j : j + 1, :], (8, n))
    for g in range(groups):
        if g == groups // 2:
            middle()
        cols = [[lane(a[h], 8 * g + l) for l in range(8)] for h in range(g, groups)]
        for j in range(8):
            scale = lax.rsqrt(row(cols[0][j], j))
            a_row = row(a[g], j) * scale
            m_row = row(m[g], j) * scale
            heads = [row(cols[0][l], j) * scale for l in range(j + 1, 8)]
            for h in range(g, groups):
                c = cols[h - g][j] * scale
                if h == g:
                    below = jnp.where(rows > j, c, 0.0)
                    a[h] = jnp.where(rows == j, a_row, a[h] - below * a_row)
                    m[h] = jnp.where(rows == j, m_row, m[h] - below * m_row)
                else:
                    a[h] = a[h] - c * a_row
                    m[h] = m[h] - c * m_row
                for l in range(j + 1, 8):
                    cols[h - g][l] = cols[h - g][l] - c * heads[l - j - 1]
    upper = jnp.concatenate(a, axis=0)
    inverse = jnp.concatenate(m, axis=0)
    r = lax.broadcasted_iota(jnp.int32, (n, n), 0)
    c = lax.broadcasted_iota(jnp.int32, (n, n), 1)
    return jnp.where(r <= c, upper, 0.0).T, jnp.where(r >= c, inverse, 0.0)


def bit(value, b):
    return lax.rem(value // (2**b), 2)


def all_of(conditions):
    return functools.reduce(jnp.logical_and, conditions)


def plan(rows_count, cols_count, tile_rows, tile_cols):
    need = [min(tile_cols, (rows_count * (a + 1) - 1) // cols_count + 1) for a in range(tile_rows)]
    return need, [(a, b) for a in range(tile_rows) for b in range(1, need[a])]


def kernel(
    rows_count, cols_count,
    matrix, checksum, flag,
    work_out, totals_out,
    own, totals, work, new_totals,
    flags, gathered, panel, lead, factor, inverses, inv_tile, cross, sums,
    left_in, right_in, left_out, right_out, low_high, low_low, front, column,
    load_sem, load_totals_sem, load_front_sem, store_sem, store_totals_sem,
    flag_send, flag_recv, gather_send, gather_recv, scan_send, scan_recv, cast_send, cast_recv,
):
    tile_rows, tile_cols, width, _ = totals.shape
    p, q = lax.axis_index("row"), lax.axis_index("col")
    last = cols_count - 1
    bits = rows_count.bit_length() - 1
    need, tiles = plan(rows_count, cols_count, tile_rows, tile_cols)
    ratio = rows_count // cols_count
    wide = PANELS * width
    places = [(a, b) for a in range(tile_rows) for b in range(need[a])]

    def load_front(a):
        return pltpu.make_async_copy(matrix.at[a, :, 0, 0, :], gathered.at[q, a], load_front_sem.at[a])

    def load_totals(a):
        return pltpu.make_async_copy(checksum.at[a], totals.at[a], load_totals_sem.at[a])

    def load_own(t):
        a, b = tiles[t]
        return pltpu.make_async_copy(matrix.at[a, :, b, 0, :], own.at[t], load_sem.at[t])

    def store_totals(b):
        return pltpu.make_async_copy(new_totals.at[b], totals_out.at[b], store_totals_sem.at[b])

    def store_work(i):
        return pltpu.make_async_copy(work.at[i], work_out.at[i], store_sem.at[i])

    load_front(0).start()
    load_totals(0).start()
    for a in range(1, tile_rows):
        load_front(a).start()
        load_totals(a).start()
    for t in range(len(tiles)):
        load_own(t).start()

    barrier = pltpu.get_barrier_semaphore()
    for o in range(cols_count):
        @pl.when(q != o)
        def _():
            pl.semaphore_signal(barrier, inc=1, device_id=(p, jnp.int32(o)), device_id_type=MESH)
    partners = [p + (1 - 2 * bit(p, b)) * (2**b) for b in range(bits)]
    for partner in partners:
        pl.semaphore_signal(barrier, inc=1, device_id=(partner, q), device_id_type=MESH)
    pl.semaphore_wait(barrier, cols_count - 1 + bits)

    def remote(src, dst, send, recv, to):
        return pltpu.make_async_remote_copy(
            src_ref=src, dst_ref=dst, send_sem=send, recv_sem=recv, device_id=to, device_id_type=MESH
        )

    def flag_copy(o):
        return remote(flag, flags, flag_send.at[o], flag_recv, (p, jnp.int32(o)))

    def flag_start():
        @pl.when(q == 0)
        def _():
            for o in range(1, cols_count):
                flag_copy(o).start()
            flags[...] = flag[...]

    def flag_wait():
        @pl.when(q != 0)
        def _():
            flag_copy(0).wait_recv()

    def lost_is(index, shape):
        return jnp.broadcast_to(flags[0:1, 0:1], shape) == index

    sides = (0, 1)
    ahead = [jnp.minimum(q + 1, last), jnp.maximum(q - 1, 0)]

    def gather_copy(side, step, a, origin):
        at = gathered.at[origin, a]
        return remote(at, at, gather_send.at[side, step, a], gather_recv.at[side, step, a], (p, ahead[side]))

    def gather_sends(side, step):
        if side == 0:
            return jnp.logical_and(q - step >= 0, q < last), jnp.maximum(q - step, 0)
        return jnp.logical_and(q + step <= last, q > 0), jnp.minimum(q + step, last)

    def gather_gets(side, step):
        if side == 0:
            return q - 1 - step >= 0, jnp.maximum(q - 1 - step, 0)
        return q + 1 + step <= last, jnp.minimum(q + 1 + step, last)

    def gather_start(step, a):
        for side in sides:
            does, origin = gather_sends(side, step)
            @pl.when(does)
            def _():
                gather_copy(side, step, a, origin).start()

    def gather_wait(step, a):
        for side in sides:
            does, origin = gather_gets(side, step)
            @pl.when(does)
            def _():
                gather_copy(side, step, a, origin).wait_recv()

    def rebuild_panel(a):
        shape = (width, width)
        others = jnp.zeros(shape, F32)
        for o in range(cols_count):
            others = others + jnp.where(lost_is(o, shape), 0.0, gathered[o, a])
        patch = totals[a, 0] - others
        for k in range(PANELS):
            panel[a, :, k * width : (k + 1) * width] = jnp.where(lost_is(k, shape), patch, gathered[k, a])
        front[a] = jnp.where(lost_is(q, shape), patch, gathered[q, a])

    forth = [b for b in range(1, bits)] + [0]
    back = [b for b in range(bits - 1, 0, -1)] + [0]

    class Cast:
        def __init__(self, number, buffer, source, order):
            self.number, self.buffer, self.order = number, buffer, order
            self.apart = [lax.rem(bit(p, b) + bit(source, b), 2) for b in range(bits)]
            self.is_source = p == source

        def copy(self, t):
            return remote(
                self.buffer, self.buffer, cast_send.at[self.number, t], cast_recv.at[self.number],
                (partners[self.order[t]], q),
            )

        def holds(self, t):
            return all_of([self.apart[b] == 0 for b in self.order[t:]])

        def gets(self, t):
            return all_of(
                [self.apart[self.order[t]] == 1] + [self.apart[b] == 0 for b in self.order[t + 1 :]]
            )

        def start(self, t):
            @pl.when(self.holds(t))
            def _():
                self.copy(t).start()

        def wait(self, t):
            @pl.when(self.gets(t))
            def _():
                self.copy(t).wait_recv()

        def finish(self):
            for t in range(bits):
                @pl.when(self.holds(t))
                def _():
                    self.copy(t).wait_send()

    number = iter(range(99))
    def lead_cast(i, k):
        at = lead.at[i * width : (i + 1) * width, k * width : (k + 1) * width]
        return Cast(next(number), at, jnp.int32(i), forth if k else back)

    lead_first = [lead_cast(i, 0) for i in range(PANELS)]
    lead_later = [lead_cast(i, k) for k in range(1, PANELS) for i in range(k, PANELS)]
    orders = (forth, back)
    half = width // 2
    sum_casts = [
        Cast(next(number), sums.at[k * width + h * half : k * width + (h + 1) * half], jnp.int32(k), orders[h])
        for k in range(PANELS)
        for h in range(2)
    ]
    cross_casts = [
        [
            Cast(next(number), cross.at[m, a, h * half : (h + 1) * half], q + cols_count * m, orders[h])
            for m in range(ratio)
            for h in range(2)
        ]
        for a in range(tile_rows)
    ]

    def cast_start(casts, t):
        for cast in casts:
            cast.start(t)

    def cast_wait(casts, t):
        for cast in casts:
            cast.wait(t)

    def lead_stage():
        for i, cast in enumerate(lead_first):
            @pl.when(cast.is_source)
            def _():
                top = slice(0, (i + 1) * width)
                lead[i * width : (i + 1) * width, top] = panel[0, :, top]

    def sum_stage():
        for k, cast in enumerate(sum_casts[::2]):
            @pl.when(cast.is_source)
            def _():
                for b in range(tile_cols):
                    sums[k * width : (k + 1) * width, b * width : (b + 1) * width] = totals[0, b]

    def cross_begin(a):
        for m, cast in enumerate(cross_casts[a][::2]):
            @pl.when(cast.is_source)
            def _():
                cross[m, a] = panel[a]
        cast_start(cross_casts[a], 0)

    scan_in, scan_out = (left_in, right_in), (left_out, right_out)
    scan_ends = (0, last)

    count = len(tiles)
    lag = 2
    hops = (q, last - q)

    def scan_copy(side, t, src):
        return remote(src, scan_in[side].at[t], scan_send.at[side, t], scan_recv.at[side, t], (p, ahead[side]))

    def scan_below(t):
        off = jnp.int32(0)
        for i, (a, b) in enumerate(tiles):
            off = jnp.where(t == i, rows_count * a - cols_count * b, off)
        return p + off

    def scan_gets(side, t):
        return jnp.logical_and(hops[side] > 0, scan_below(t) >= (0 if side else q))

    def scan_sends(side, t):
        return jnp.logical_and(hops[side] < last, scan_below(t) >= (0 if side else q + 1))

    def scan_tick(n):
        for side in sides:
            hop = hops[side]
            t = n - lag * hop
            busy = jnp.logical_and(t >= 0, t < count)
            t = jnp.clip(t, 0, count - 1)
            busy = jnp.logical_and(busy, scan_sends(side, t))

            @pl.when(jnp.logical_and(busy, hop == 0))
            def _():
                scan_copy(side, t, own.at[t]).start()

            @pl.when(jnp.logical_and(busy, hop > 0))
            def _():
                copy = scan_copy(side, t, scan_out[side].at[t])
                copy.wait_recv()
                scan_out[side][t] = scan_in[side][t] + own[t]
                copy.start()

    def scan_last(t):
        for side in sides:
            @pl.when(jnp.logical_and(scan_gets(side, t), jnp.logical_not(scan_sends(side, t))))
            def _():
                scan_copy(side, t, scan_out[side].at[t]).wait_recv()
            @pl.when(q == scan_ends[side])
            def _():
                scan_in[side][t] = jnp.zeros((width, width), F32)

    def finish():
        @pl.when(q == 0)
        def _():
            for o in range(1, cols_count):
                flag_copy(o).wait_send()
        for step in range(last):
            for a in range(tile_rows):
                for side in sides:
                    does, origin = gather_sends(side, step)
                    @pl.when(does)
                    def _():
                        gather_copy(side, step, a, origin).wait_send()
        for t in range(len(tiles)):
            for side in sides:
                @pl.when(scan_sends(side, t))
                def _():
                    scan_copy(side, t, scan_out[side].at[t]).wait_send()
        for cast in lead_first + lead_later + sum_casts + sum(cross_casts, []):
            cast.finish()

    factor[...] = jnp.zeros_like(factor)
    rest = range(1, tile_rows)
    flag_start()
    load_front(0).wait()
    gather_start(0, 0)
    load_totals(0).wait()
    sum_stage()
    cast_start(sum_casts, 0)
    def rest_start():
        for a in rest:
            gather_start(0, a)

    for step in range(last):
        gather_wait(step, 0)
        if step + 1 < last:
            gather_start(step + 1, 0)
        if step == 0:
            for a in rest:
                load_front(a).wait()

            @pl.when(p > PANELS)
            def _():
                rest_start()


    @pl.when(p <= PANELS)
    def _():
        rest_start()

    flag_wait()
    rebuild_panel(0)
    lead_stage()
    cast_start(lead_first + lead_later, 0)
    for t in range(count):
        load_own(t).wait()
    scan_tick(0)

    def cast_step(casts, t):
        cast_wait(casts, t)
        if t + 1 < bits:
            cast_start(casts, t + 1)

    def gather_step(step):
        for a in rest:
            gather_wait(step, a)
            if step + 1 < last:
                gather_start(step + 1, a)

    for t in range(bits - 1):
        cast_step(lead_first, t)
        cast_step(lead_later, t)
    cast_wait(lead_first, bits - 1)
    cast_step(sum_casts, 0)
    cross_begin(0)

    def panel_ready(a):
        load_totals(a).wait()
        rebuild_panel(a)
        cross_begin(a)

    blocks = wide // BLOCK
    service = {point: [] for point in range(2 * blocks)}
    service[0] += [lambda: gather_step(0)]
    service[1] += [lambda: gather_step(1)]
    service[2] += [lambda step=step: gather_step(step) for step in range(2, last)]
    service[2] += [lambda a=a: panel_ready(a) for a in rest]
    service[8] += [lambda: cast_step(sum_casts, 1)]
    service[5] += [lambda: cast_step(cross_casts[0], 0)]
    service[8] += [lambda a=a: cast_step(cross_casts[a], 0) for a in rest]
    service[10] += [lambda: cast_step(cross_casts[0], 1)]
    service[4] = [lambda: cast_wait(lead_later, bits - 1)] + service[4]
    ticks_at = (0, 2, 4, 6, 8, 10)
    first_tick = 1

    def serve(n, at):
        for point in range(at, 2 * blocks, 2):
            if service[point]:
                @pl.when(2 * n + at == point)
                def _():
                    for action in service[point]:
                        action()
        done = jnp.int32(first_tick)
        now = jnp.int32(0)
        for point in ticks_at:
            done = done + jnp.where(2 * n + at > point, 1, 0)
            now = now + jnp.where(2 * n + at == point, 1, 0)

        @pl.when(now > 0)
        def _():
            scan_tick(done)


    def column_update(k):
        low, high = k * width, (k + 1) * width
        value = lead[low:, low:high]
        if k:
            value = value - exact_dot(factor[low:, :low], factor[low:high, :low], 1, 1)
        column[low:, :] = value

    def below_update(n, lower, inverse):
        low, high = n * BLOCK, (n + 1) * BLOCK
        at = n % 2 * BLOCK
        factor[low:high, low:high] = lower
        if high < wide:
            below = exact_dot(column[high:, at : at + BLOCK], inverse, 1, 1)
            factor[high:, low:high] = below
            if n % 2 == 0:
                column[high:, BLOCK:] = column[high:, BLOCK:] - exact_dot(below, below[:BLOCK], 1, 1)

    def factor_step(n, carry):
        serve(n, 0)
        for k in range(PANELS):
            @pl.when(n == 2 * k)
            def _():
                column_update(k)
        o = pl.multiple_of(n * BLOCK, BLOCK)
        at = pl.multiple_of(lax.rem(n, 2) * BLOCK, BLOCK)
        lower, inverse = factor_block(column[pl.ds(o, BLOCK), pl.ds(at, BLOCK)], lambda: serve(n, 1))
        inverses[n] = inverse
        for block in range(blocks):
            @pl.when(n == block)
            def _():
                below_update(block, lower, inverse)
        return carry

    lax.fori_loop(0, blocks, factor_step, 0)

    for k in range(PANELS):
        one, two = inverses[2 * k], inverses[2 * k + 1]
        corner = factor[k * width + BLOCK : (k + 1) * width, k * width : k * width + BLOCK]
        inv_tile[k, :BLOCK, :BLOCK] = one
        inv_tile[k, :BLOCK, BLOCK:] = jnp.zeros((BLOCK, BLOCK), F32)
        inv_tile[k, BLOCK:, :BLOCK] = -exact_dot(two, exact_dot(corner, one, 1, 0), 1, 0)
        inv_tile[k, BLOCK:, BLOCK:] = two

    def part(i, m):
        return split(factor[i * width : (i + 1) * width, m * width : (m + 1) * width])

    def solve_rows(x):
        solved = []
        for k in range(PANELS):
            y = x[:, k * width : (k + 1) * width]
            for m in range(k):
                y = y - dot3(split(solved[m]), part(k, m), 1, 1)
            solved.append(dot3(split(y), split(inv_tile[k]), 1, 1))
        return jnp.concatenate(solved, axis=1)

    row_tile = [p + a * rows_count for a in range(tile_rows)]

    tick = first_tick + len(ticks_at)
    scan_tick(tick)
    solved_rows = solve_rows(panel[...].reshape(tile_rows * width, wide))
    for a in range(tile_rows):
        x = solved_rows[a * width : (a + 1) * width]
        if a == 0:
            top = factor[pl.ds(pl.multiple_of(jnp.minimum(p, PANELS - 1) * width, width), width), :]
            x = jnp.where(jnp.broadcast_to(p, x.shape) < PANELS, top, x)
        panel[a] = x
        low_high[a], low_low[a] = split(x)
    scan_tick(tick + 1)
    tick += 2

    def low_rows(a):
        count_rows = (tile_rows - a) * width
        return low_high[a:].reshape(count_rows, wide), low_low[a:].reshape(count_rows, wide)

    for t in range(2, bits):
        cast_step(sum_casts, t)
    for a in rest:
        cast_step(cross_casts[a], 1)

    group = 1 + (tile_cols + 1) % 2

    def sums_body(n, carry):
        scan_tick(tick + n)
        at = pl.ds(pl.multiple_of(n * group * width, width), group * width)
        solved = []
        for k in range(PANELS):
            y = sums[k * width : (k + 1) * width, at]
            for m in range(k):
                y = y - dot3(part(k, m), solved[m], 1, 0)
            solved.append(split(dot3(split(inv_tile[k]), split(y), 1, 0)))
        y = (jnp.concatenate([s[0] for s in solved], 0), jnp.concatenate([s[1] for s in solved], 0))
        drop = dot3(low_rows(0), y, 1, 0)
        for g in range(group):
            b = n * group + g
            for a in range(tile_rows):
                new_totals[b, a] = totals[a, b] - drop[a * width : (a + 1) * width, g * width : (g + 1) * width]
            store_totals(b).start()
        return carry

    lax.fori_loop(0, tile_cols // group, sums_body, 0)
    tick += tile_cols // group

    for a_from in range(tile_rows):
        scan_tick(tick + a_from)
        for t in range(2, bits):
            cast_step(cross_casts[a_from], t)
        y = split(solve_rows(cross[:, a_from].reshape(ratio * width, wide)))
        value = dot3(low_rows(a_from), y, 1, 1)
        for a in range(a_from, tile_rows):
            for m in range(ratio):
                rows = slice((a - a_from) * width, (a - a_from + 1) * width)
                work[places.index((a, m + ratio * a_from))] = value[rows, m * width : (m + 1) * width]
    tick += tile_rows
    ticks = count + lag * (last - 1)

    def tick_body(n, carry):
        scan_tick(n)
        return carry

    if ticks > tick:
        lax.fori_loop(tick, ticks, tick_body, 0)
    shape = (width, width)
    for i, (a, b) in enumerate(places):
        if b == 0:
            value = front[a] - work[i]
            for k in range(PANELS):
                value = jnp.where(
                    jnp.broadcast_to(q, shape) == k, panel[a, :, k * width : (k + 1) * width], value
                )
        else:
            t = tiles.index((a, b))
            scan_last(t)
            back_in = totals[a, b] - (left_in[t] + right_in[t])
            value = jnp.where(lost_is(q, shape), back_in, own[t]) - work[i]
        keep = jnp.broadcast_to(row_tile[a], shape) >= jnp.broadcast_to(q + b * cols_count, shape)
        work[i] = jnp.where(keep, value, 0.0)
        store_work(i).start()
    for i in range(len(places)):
        store_work(i).wait()
    for b in range(tile_cols):
        store_totals(b).wait()
    finish()


def place_kernel(places, work, totals, work_out, totals_out, held, zero, held_totals, load, store, load_t, store_t):
    cols, rows = totals.shape[:2]
    loads = [pltpu.make_async_copy(work.at[i], held.at[i], load.at[i]) for i in range(len(places))]
    loads_t = [pltpu.make_async_copy(totals.at[b], held_totals.at[b], load_t.at[b]) for b in range(cols)]
    for copy in loads + loads_t:
        copy.start()
    zero[...] = jnp.zeros_like(zero)
    stores = []
    for a in range(rows):
        for b in range(cols):
            to = work_out.at[a, :, b, 0, :]
            if (a, b) not in places:
                stores.append(pltpu.make_async_copy(zero, to, store.at[a, b]))
                stores[-1].start()
    for i, (a, b) in enumerate(places):
        loads[i].wait()
        stores.append(pltpu.make_async_copy(held.at[i], work_out.at[a, :, b, 0, :], store.at[a, b]))
        stores[-1].start()
    for b in range(cols):
        loads_t[b].wait()
        for a in range(rows):
            stores.append(pltpu.make_async_copy(held_totals.at[b, a], totals_out.at[a, b], store_t.at[a, b]))
            stores[-1].start()
    for copy in stores:
        copy.wait()


def shards(matrix, checksum, failed):
    rows_count, cols_count = lax.axis_size("row"), lax.axis_size("col")
    tile_rows, width, tile_cols = matrix.shape[1], matrix.shape[2], matrix.shape[4]
    assert width == 2 * BLOCK and rows_count % cols_count == 0
    assert cols_count >= PANELS and rows_count & (rows_count - 1) == 0
    own = matrix.reshape(tile_rows, width, tile_cols, 1, width)
    totals = checksum.reshape(tile_rows, width, tile_cols, width).transpose(0, 2, 1, 3)
    flag = jnp.broadcast_to(failed.reshape(1, 1), (8, 128))
    wide = PANELS * width
    bits = rows_count.bit_length() - 1
    ratio = rows_count // cols_count
    need, tiles = plan(rows_count, cols_count, tile_rows, tile_cols)
    count = len(tiles)
    casts = PANELS * (PANELS + 1) // 2 + 2 * PANELS + 2 * ratio * tile_rows
    vmem = pl.BlockSpec(memory_space=pltpu.VMEM)
    dma = pltpu.SemaphoreType.DMA
    hbm = pl.BlockSpec(memory_space=pl.ANY)
    places = [(a, b) for a in range(tile_rows) for b in range(need[a])]
    tile = lambda *n: pltpu.VMEM((*n, width, width), F32)
    shape = lambda *n: jax.ShapeDtypeStruct((*n, width, width), F32)
    work, new_totals = pl.pallas_call(
        functools.partial(kernel, rows_count, cols_count),
        out_shape=[shape(len(places)), shape(tile_cols, tile_rows)],
        in_specs=[hbm, hbm, vmem],
        out_specs=[hbm, hbm],
        scratch_shapes=[
            tile(count),
            tile(tile_rows, tile_cols),
            tile(len(places)),
            tile(tile_cols, tile_rows),
            pltpu.VMEM((8, 128), jnp.int32),
            pltpu.VMEM((cols_count, tile_rows, width, width), F32),
            pltpu.VMEM((tile_rows, width, wide), F32),
            pltpu.VMEM((wide, wide), F32),
            pltpu.VMEM((wide, wide), F32),
            pltpu.VMEM((wide // BLOCK, BLOCK, BLOCK), F32),
            pltpu.VMEM((PANELS, width, width), F32),
            pltpu.VMEM((ratio, tile_rows, width, wide), F32),
            pltpu.VMEM((wide, tile_cols * width), F32),
        ]
        + [pltpu.VMEM((count, width, width), F32)] * 4
        + [pltpu.VMEM((tile_rows, width, wide), BF16)] * 2
        + [pltpu.VMEM((tile_rows, width, width), F32), pltpu.VMEM((wide, width), F32)]
        + [
            dma((count,)),
            dma((tile_rows,)),
            dma((tile_rows,)),
            dma((len(places),)),
            dma((tile_cols,)),
            dma((cols_count,)),
            dma,
            dma((2, cols_count - 1, tile_rows)),
            dma((2, cols_count - 1, tile_rows)),
            dma((2, count)),
            dma((2, count)),
            dma((casts, bits)),
            dma((casts,)),
        ],
        compiler_params=pltpu.CompilerParams(
            collective_id=0, has_side_effects=True, vmem_limit_bytes=62 * 2**20
        ),
        cost_estimate=pl.CostEstimate(flops=30 * 10**9, bytes_accessed=20 * 10**6, transcendentals=0),
    )(own, totals, flag)
    work, new_totals = pl.pallas_call(
        functools.partial(place_kernel, places),
        out_shape=[jax.ShapeDtypeStruct(own.shape, F32), shape(tile_rows, tile_cols)],
        in_specs=[hbm, hbm],
        out_specs=[hbm, hbm],
        scratch_shapes=[
            tile(len(places)),
            tile(),
            tile(tile_cols, tile_rows),
            dma((len(places),)),
            dma((tile_rows, tile_cols)),
            dma((tile_cols,)),
            dma((tile_rows, tile_cols)),
        ],
        compiler_params=pltpu.CompilerParams(vmem_limit_bytes=62 * 2**20),
        cost_estimate=pl.CostEstimate(flops=0, bytes_accessed=20 * 10**6, transcendentals=0),
    )(work, new_totals)
    new_totals = new_totals.transpose(0, 2, 1, 3)
    return work.reshape(matrix.shape), new_totals.reshape(checksum.shape)


def solution(mesh):
    return jax.shard_map(
        shards,
        mesh=mesh,
        in_specs=(
            P("row", None, None, "col", None, None),
            P("row", None, None, None, None),
            P("col"),
        ),
        out_specs=(P("row", None, None, "col", None, None), P("row", None, None, None, None)),
        check_vma=False,
    )
```
